128 devices in a mesh: tiles: 128 (over y, z, x, core).
Axes of the slice: x: 4, y: 4, z: 4, core: 2. Of those that a mesh axis runs over, the one named last changes fastest.
Arguments:
- mask_param: float32 [128, 512, 512], P('tiles'), may hold values from -6 to 6
- target: bfloat16 [128, 512, 512], P('tiles'), may hold values from 0 to 1
- counts: int32 [128, 4], replicated, may hold values from 1 to 4, as said below
- kernels: float32 [4, 12, 64, 128], replicated, may hold values from -4.25 to 4.25
- weights: float32 [4, 12], replicated, may hold values from 0.1 to 1
- thresholds: float32 [4], replicated, may hold values from 0.3 to 0.6
Outputs:
- mask_out: float32 [128, 512, 512], P('tiles')
- gradient: float32 [128, 512, 512], P('tiles')
The draws below stay inside these ranges and needn't reach their ends.
Inputs may be any that keep to these rules, and one draw needn't show every extreme that they name: `counts`: blocks 0 to 63 have 2 to 4 conditions on each tile, the other blocks one condition on each tile; in every draw some block among the first 64 has 4 conditions on all its tiles.
All inputs are finite; a program needn't handle non-finite values.
Results may differ from the reference program's by a relative error of at most 0.0095.
Values may be sent and summed in bfloat16 or wider, within the bound.
A program may use at most 64 MiB of HBM per device.

```python
import math
import jax
import jax.numpy as jnp
from jax import lax

TILE = 256
HALO = 32
KF = 64
KERNELS = 12
CONDS = 4
DEV_COLS = 8
ITERS = 1
TPD = 4
BH = 512
BW = 512
BLOCKS = 128


def draw_counts(key, part):
    half_blocks = BLOCKS // 2
    key_heavy, key_chosen = jax.random.split(jax.random.fold_in(key, 17))
    heavy = jax.random.randint(key_heavy, (BLOCKS, TPD), 2, 5)
    chosen = jax.random.randint(key_chosen, (), 0, half_blocks)
    block_ids = jnp.arange(BLOCKS)[:, None]
    heavy = jnp.where(block_ids == chosen, 4, heavy)
    return jnp.where(block_ids < half_blocks, heavy, 1).astype(jnp.int32)


def block_scale(rng, shape, cuts, least, high):
    def one(axis_at, parts):
        draws = jax.random.uniform(jax.random.fold_in(jax.random.fold_in(rng, 6), axis_at), (parts,), jnp.float32, least / len(cuts), high / len(cuts))
        return jnp.repeat(jnp.exp(draws), shape[axis_at] // parts).reshape((-1,) + (1,) * (len(shape) - axis_at - 1))

    factor_of = one(*cuts[0])
    for cut in cuts[1:]:
        factor_of = factor_of * one(*cut)
    return factor_of


def centred(key, dims, deviation, most, pieces=(), held_as=jnp.bfloat16):
    level = block_scale(key, dims, pieces, -0.22, 0.18) if pieces else 1.0
    entries = jax.random.normal(key, dims, jnp.float32) * deviation * level
    return jnp.minimum(jnp.maximum(entries, -most), most).astype(held_as)


def setup_inputs(seed: int = 0) -> dict:
    arg_keys = jax.random.split(jax.random.key(seed), 7)
    return {
        "mask_param": centred(arg_keys[0], (BLOCKS, BH, BW), 1.0, 6.0, ((0, 128),), jnp.float32),
        "target": jnp.clip(1.0 * jax.random.uniform(arg_keys[1], (BLOCKS, BH, BW), jnp.float32) ** block_scale(arg_keys[1], (BLOCKS, BH, BW), ((0, 128),), -0.2, 0.2), 0.0, 1.0).astype(jnp.bfloat16),
        "counts": draw_counts(jax.random.fold_in(arg_keys[6], 71), 0),
        "kernels": centred(arg_keys[3], (CONDS, KERNELS, KF, 2 * KF), 0.7071, 4.25, (), jnp.float32),
        "weights": jnp.clip(jnp.exp(jax.random.uniform(arg_keys[4], (CONDS, KERNELS), jnp.float32, math.log(0.1), math.log(1.0))), 0.1, 1.0),
        "thresholds": jnp.clip(jax.random.uniform(arg_keys[5], (CONDS,), jnp.float32, 0.3, 0.6), 0.3, 0.6),
    }


STEEPNESS = 8.0
STEP_SIZE = 0.25
PRECISE_DOT = lax.Precision.HIGHEST


def rounded(values):
    return lax.optimization_barrier(values.astype(jnp.bfloat16)).astype(jnp.float32)


def make_tables(tile_px, margin, freq_count):
    padded = tile_px + 2 * margin
    offsets = jnp.arange(freq_count, dtype=jnp.float32) - freq_count // 2
    pixels = jnp.arange(padded, dtype=jnp.float32)
    angles = 2.0 * jnp.pi * offsets[:, None] * pixels[None, :] / padded
    forward_tab = rounded(jnp.concatenate([jnp.cos(angles), jnp.sin(angles)], 0))
    inner_px = jnp.arange(tile_px, dtype=jnp.float32) + margin
    inner_angles = 2.0 * jnp.pi * inner_px[:, None] * offsets[None, :] / padded
    inverse_tab = rounded(jnp.stack([jnp.cos(inner_angles), jnp.sin(inner_angles)]))
    return forward_tab, inverse_tab


def spectrum_ref(window, forward_tab):
    freq_count = forward_tab.shape[0] // 2
    halves = rounded(jnp.dot(window, forward_tab.T, precision=PRECISE_DOT))
    products = jnp.dot(forward_tab, halves, precision=PRECISE_DOT)
    real_part = products[:freq_count, :freq_count] - products[freq_count:, freq_count:]
    imag_part = -(products[:freq_count, freq_count:] + products[freq_count:, :freq_count])
    return jnp.concatenate([real_part, imag_part], 1)


def adjoint_ref(grad_spec, forward_tab):
    freq_count = forward_tab.shape[0] // 2
    real_part = grad_spec[:, :freq_count]
    imag_part = grad_spec[:, freq_count:]
    top_rows = jnp.concatenate([real_part, -imag_part], 1)
    low_rows = jnp.concatenate([-imag_part, -real_part], 1)
    grad_whole = jnp.concatenate([top_rows, low_rows], 0)
    grad_halves = rounded(jnp.dot(forward_tab.T, grad_whole, precision=PRECISE_DOT))
    return jnp.dot(grad_halves, forward_tab, precision=PRECISE_DOT)


def unit_gradient(spectrum, kern_pair, weight_row, threshold, target_tile, inverse_tab, norm_scale):
    freq_count = spectrum.shape[0]
    spec_re = spectrum[:, :freq_count]
    spec_im = spectrum[:, freq_count:]
    kern_re = kern_pair[:, :, :freq_count]
    kern_im = kern_pair[:, :, freq_count:]
    mixed_spec = rounded(jnp.stack([kern_re * spec_re - kern_im * spec_im, kern_re * spec_im + kern_im * spec_re], 1))
    row_prod = jnp.einsum('kafm,bym->kafby', mixed_spec, inverse_tab, precision=PRECISE_DOT)
    row_half = rounded(jnp.stack([row_prod[:, 0, :, 0] - row_prod[:, 1, :, 1], row_prod[:, 0, :, 1] + row_prod[:, 1, :, 0]], 1))
    field_parts = jnp.einsum('bxf,kafy->kbaxy', inverse_tab, row_half, precision=PRECISE_DOT) * norm_scale
    field_re = field_parts[:, 0, 0] - field_parts[:, 1, 1]
    field_im = field_parts[:, 0, 1] + field_parts[:, 1, 0]
    intensity = jnp.sum(weight_row[:, None, None] * (field_re * field_re + field_im * field_im), 0)
    resist = jax.nn.sigmoid(STEEPNESS * (intensity - threshold))
    grad_int = 2.0 * (resist - target_tile) * STEEPNESS * resist * (1.0 - resist)
    scaled = 2.0 * weight_row[:, None, None] * grad_int[None]
    grad_field = rounded(jnp.stack([scaled * field_re, scaled * field_im], 1))
    grad_prod = jnp.einsum('bxf,kaxy->kbafy', inverse_tab, grad_field, precision=PRECISE_DOT) * norm_scale
    grad_half = rounded(jnp.stack([grad_prod[:, 0, 0] + grad_prod[:, 1, 1], grad_prod[:, 0, 1] - grad_prod[:, 1, 0]], 1))
    grad_mix = jnp.einsum('kafy,bym->kabfm', grad_half, inverse_tab, precision=PRECISE_DOT)
    grad_re = grad_mix[:, 0, 0] + grad_mix[:, 1, 1]
    grad_im = grad_mix[:, 1, 0] - grad_mix[:, 0, 1]
    out_re = jnp.sum(kern_re * grad_re + kern_im * grad_im, 0)
    out_im = jnp.sum(kern_re * grad_im - kern_im * grad_re, 0)
    return jnp.concatenate([out_re, out_im], 1)


def reference(mask_param, target, counts, kernels, weights, thresholds):
    grid_rows = BLOCKS // DEV_COLS
    padded = TILE + 2 * HALO
    tile_rows = BH // TILE
    tile_cols = BW // TILE
    per_block = tile_rows * tile_cols
    norm_scale = 1.0 / (padded * KF)
    forward_tab, inverse_tab = make_tables(TILE, HALO, KF)
    levels = mask_param.reshape(grid_rows, DEV_COLS, BH, BW).transpose(0, 2, 1, 3).reshape(grid_rows * BH, DEV_COLS * BW)
    target_all = target.astype(jnp.float32)
    tile_ids = jnp.arange(BLOCKS * per_block, dtype=jnp.int32)
    gradient = jnp.zeros_like(levels)
    for iteration in range(ITERS):
        opening = jax.nn.sigmoid(levels)
        transmit = jnp.pad(2.0 * opening - 1.0, HALO)

        def add_tile(canvas, tile_id):
            block_id = tile_id // per_block
            within = tile_id % per_block
            row_tile = within // tile_cols
            col_tile = within % tile_cols
            top_row = (((block_id // DEV_COLS) * tile_rows + row_tile) * TILE).astype(jnp.int32)
            left_col = (((block_id % DEV_COLS) * tile_cols + col_tile) * TILE).astype(jnp.int32)
            window = rounded(lax.dynamic_slice(transmit, (top_row, left_col), (padded, padded)))
            spectrum = rounded(spectrum_ref(window, forward_tab))
            target_tile = lax.dynamic_slice(target_all, (block_id.astype(jnp.int32), (row_tile * TILE).astype(jnp.int32), (col_tile * TILE).astype(jnp.int32)), (1, TILE, TILE))[0]

            def add_cond(cond_id, running):
                return running + unit_gradient(spectrum, kernels[cond_id], weights[cond_id], thresholds[cond_id], target_tile, inverse_tab, norm_scale)

            grad_spec = lax.fori_loop(jnp.int32(0), counts[block_id, within].astype(jnp.int32), add_cond, jnp.zeros((KF, 2 * KF), jnp.float32))
            grad_window = adjoint_ref(rounded(grad_spec), forward_tab)
            current = lax.dynamic_slice(canvas, (top_row, left_col), (padded, padded))
            return lax.dynamic_update_slice(canvas, current + grad_window, (top_row, left_col)), None

        canvas, unused = lax.scan(add_tile, jnp.zeros(transmit.shape, jnp.float32), tile_ids)
        gradient = canvas[HALO:-HALO, HALO:-HALO] * 2.0 * opening * (1.0 - opening)
        levels = levels - STEP_SIZE * gradient
    mask_out = levels.reshape(grid_rows, BH, DEV_COLS, BW).transpose(0, 2, 1, 3).reshape(BLOCKS, BH, BW)
    grad_out = gradient.reshape(grid_rows, BH, DEV_COLS, BW).transpose(0, 2, 1, 3).reshape(BLOCKS, BH, BW)
    return mask_out, grad_out
```

```python
import functools

import jax
import jax.numpy as jnp
import ml_dtypes
import numpy as np
from jax import lax
from jax.experimental import pallas as pl
from jax.experimental.pallas import tpu as pltpu
from jax.sharding import PartitionSpec as P

TILE = 256
HALO = 32
KF = 64
DEV_COLS = 8
PADDED = TILE + 2 * HALO
COARSE = 2 * KF
NK = 12
CONDS = 4
STEEPNESS = 8.0
STEP_SIZE = 0.25
SCALE = 1.0 / (PADDED * KF)

F32 = jnp.float32
BF16 = jnp.bfloat16
MESH = pl.DeviceIdType.MESH
WAYS = [(dr, dc) for dr in (-1, 0, 1) for dc in (-1, 0, 1) if (dr, dc) != (0, 0)]


def bf(values):
    return np.asarray(values, np.float32).astype(ml_dtypes.bfloat16)


def edge_table():
    freq = np.arange(KF) - KF // 2
    pixels = np.arange(PADDED)
    angles = 2.0 * np.pi * freq[:, None] * pixels[None, :] / PADDED
    forward = np.concatenate([np.cos(angles), np.sin(angles)], 0)
    table = np.zeros((2 * TILE, 4 * 2 * KF))
    for slot in range(4):
        first = (slot - 1) * TILE - HALO
        for pixel in range(2 * TILE):
            if 0 <= pixel - first < PADDED:
                table[pixel, slot * 2 * KF : (slot + 1) * 2 * KF] = forward[:, pixel - first]
    return bf(table)


def unit_tables():
    freq = np.arange(KF) - KF // 2
    angles = 2.0 * np.pi * np.arange(COARSE)[:, None] * freq[None, :] / COARSE
    cos_t, sin_t = np.cos(angles), np.sin(angles)
    t1 = np.block([[cos_t.T, sin_t.T], [-sin_t.T, cos_t.T]])
    t2 = np.block([[cos_t, -sin_t], [sin_t, cos_t]])
    shift = (np.arange(TILE) + HALO)[:, None] - PADDED / COARSE * np.arange(COARSE)[None, :]
    waves = np.arange(1, COARSE // 2)
    interp = (
        1.0 + 2.0 * np.cos(2.0 * np.pi * shift[:, :, None] * waves / PADDED).sum(-1)
    ) / COARSE
    up_hi = bf(interp)
    up_lo = bf(interp - up_hi.astype(np.float64))
    return np.concatenate(
        [
            bf(t1),
            bf(t2.T),
            up_hi.T,
            np.concatenate([up_hi, up_hi], 1),
            np.concatenate([up_hi.T, up_hi.T, up_lo.T], 0),
            np.concatenate([bf(t2), bf(t1.T)], 1),
            np.concatenate([up_lo, up_hi], 1),
        ],
        0,
    )


EDGE = edge_table()
EDGE_T = np.ascontiguousarray(EDGE.T)
UNIT = unit_tables()


def dot(a, b):
    return jnp.dot(a, b, preferred_element_type=F32)


def swap_pair(v):
    return jnp.concatenate(
        [
            jnp.concatenate([v[:64, :128], v[64:, :128]], 1),
            jnp.concatenate([v[:64, 128:], v[64:, 128:]], 1),
        ],
        0,
    )


def low_half(shape):
    return lax.broadcasted_iota(jnp.int32, shape, 1) < KF


def gradient_kernel(
    counts, weights, thresholds, mask, target, kernels, edge, edge_t, unit,
    out,
    levels, pixels, halves, part, got, spec, tgt, kraw, kre, kim, fields, acc, gspec, shared, edge_v, edge_tv, unit_v,
    load_sem, send_sem, recv_sem,
):
    me = lax.axis_index("tiles")
    devices = lax.axis_size("tiles")
    quarter = devices // 4
    half = devices // 2
    my_col = me % DEV_COLS
    my_row = me // DEV_COLS
    grid_rows = devices // DEV_COLS
    heavy = me < half
    partner = me + (3 - 2 * (me // quarter)) * quarter

    def has(dr, dc):
        ok = (my_row + dr >= 0) & (my_row + dr < grid_rows)
        return ok & (my_col + dc >= 0) & (my_col + dc < DEV_COLS)

    def peer(dr, dc):
        return lax.rem(me + dr * DEV_COLS + dc + devices, devices)

    loads = [
        pltpu.make_async_copy(mask.at[0], levels, load_sem.at[0]),
        pltpu.make_async_copy(edge, edge_v, load_sem.at[1]),
        pltpu.make_async_copy(edge_t, edge_tv, load_sem.at[2]),
        pltpu.make_async_copy(kernels, kraw, load_sem.at[3]),
        pltpu.make_async_copy(unit, unit_v, load_sem.at[4]),
    ] + [
        pltpu.make_async_copy(
            target.at[0, pl.ds((k // 2) * TILE, TILE), pl.ds((k % 2) * TILE, TILE)],
            tgt.at[k],
            load_sem.at[5 + k],
        )
        for k in range(4)
    ]
    for load in loads:
        load.start()

    barrier = pltpu.get_barrier_semaphore()
    greeted = jnp.int32(1)
    for dr, dc in WAYS:
        greeted = greeted + has(dr, dc).astype(jnp.int32)

        @pl.when(has(dr, dc))
        def _():
            pl.semaphore_signal(barrier, inc=1, device_id=(peer(dr, dc),), device_id_type=MESH)

    pl.semaphore_signal(barrier, inc=1, device_id=(partner,), device_id_type=MESH)

    def remote(src, dst, number, to):
        return pltpu.make_async_remote_copy(
            src_ref=src,
            dst_ref=dst,
            send_sem=send_sem.at[number],
            recv_sem=recv_sem.at[number],
            device_id=(to,),
            device_id_type=MESH,
        )

    span = {-1: 0, 0: pl.ds(1, 2), 1: 3}
    back = {-1: 3, 0: pl.ds(1, 2), 1: 0}
    rim = {-1: 1, 0: pl.ds(1, 2), 1: 2}

    def spectrum_copy(number):
        dr, dc = WAYS[number]
        return remote(part.at[span[dr], span[dc]], got.at[back[dr], back[dc]], number, peer(dr, dc))

    def gradient_copy(number):
        dr, dc = WAYS[number]
        return remote(
            gspec.at[rim[dr], rim[dc]], gspec.at[back[dr], back[dc]], 8 + number, peer(dr, dc)
        )

    target_copy = remote(
        target.at[0, pl.ds(TILE, TILE), pl.ds(TILE, TILE)], tgt.at[4], 16, partner
    )
    share_copy = remote(spec.at[3], spec.at[4], 17, partner)
    result_copy = remote(shared, gspec.at[2, 2], 18, partner)

    for dr, dc in WAYS:

        @pl.when(jnp.logical_not(has(dr, dc)))
        def _():
            rows = 2 if dr == 0 else 1
            cols = 2 if dc == 0 else 1
            for i in range(rows):
                for j in range(cols):
                    a = {-1: 0, 0: 1 + i, 1: 3}[dr]
                    e = {-1: 0, 0: 1 + j, 1: 3}[dc]
                    got[a, e] = jnp.zeros((KF, 2 * KF), BF16)

    loads[0].wait()
    for r in range(4):
        rows = pl.ds(r * 128, 128)
        pixels[rows, :] = jnp.tanh(0.5 * levels[rows, :]).astype(BF16)

    pl.semaphore_wait(barrier, greeted)

    @pl.when(heavy)
    def _():
        target_copy.start()

    loads[1].wait()

    @pl.loop(0, 4)
    def _(r):
        rows = pl.ds(pl.multiple_of(r * 128, 128), 128)
        x = pixels[rows, :]
        halves[rows, 0:128] = dot(x[:, 0:128], edge_v[0:128, 0:128]).astype(BF16)
        halves[rows, 128:384] = dot(x, edge_v[:, 128:384]).astype(BF16)
        halves[rows, 384:512] = dot(x[:, 384:512], edge_v[384:512, 384:512]).astype(BF16)

    loads[2].wait()
    low = low_half((KF, 2 * KF))
    tall = {0: slice(0, 128), 1: slice(0, 384), 2: slice(128, 512), 3: slice(384, 512)}
    for a in (0, 3, 1, 2):
        prod = dot(edge_tv[a * 128 : (a + 1) * 128, tall[a]], halves[tall[a], :])
        for e in range(4):
            top = prod[:KF, e * 128 : (e + 1) * 128]
            low_rows = pltpu.roll(prod[KF:, e * 128 : (e + 1) * 128], KF, 1)
            value = jnp.where(low, top - low_rows, -(top + low_rows))
            if a in (1, 2) and e in (1, 2):
                acc[(a - 1) * 2 + e - 1] = value
            else:
                part[a, e] = value.astype(BF16)

    for number, (dr, dc) in enumerate(WAYS):

        @pl.when(has(dr, dc))
        def _():
            spectrum_copy(number).start()

    loads[3].wait()

    @pl.loop(0, CONDS)
    def _(c):
        for n in range(NK):
            k = kraw[c, n]
            amount = jnp.sqrt(jnp.full((1, 2 * KF), weights[c, n], F32)) * SCALE
            k = k * amount
            turned = pltpu.roll(k, KF, 1)
            kre[c, n * KF : (n + 1) * KF, :] = jnp.where(low, k, turned)
            kim[c, n * KF : (n + 1) * KF, :] = jnp.where(low, -turned, k)

    for load in loads[4:]:
        load.wait()

    for number, (dr, dc) in enumerate(WAYS):

        @pl.when(has(-dr, -dc))
        def _():
            spectrum_copy(number).wait_recv()

    for a in (1, 0):
        for e in (1, 0):
            oa = 3 * a
            oe = 3 * e
            total = (
                acc[a * 2 + e]
                + got[1 + a, oe].astype(F32)
                + got[oa, 1 + e].astype(F32)
                + got[oa, oe].astype(F32)
            )
            spec[a * 2 + e] = total.astype(BF16)
            acc[a * 2 + e] = jnp.zeros((KF, 2 * KF), F32)

        if a == 1:

            @pl.when(heavy)
            def _():
                share_copy.start()

    acc[4] = jnp.zeros((KF, 2 * KF), F32)

    t1 = unit_v.at[0:128, :]
    t2t = unit_v.at[128:256, :]
    upt = unit_v.at[256:384, :]
    up2 = unit_v.at[384:640, :]
    upt3 = unit_v.at[640:1024, :]
    t2 = unit_v.at[1024:1280, 0:128]
    t1t = unit_v.at[1024:1280, 128:256]
    up_lo = unit_v.at[1280:1536, 0:128]
    up = unit_v.at[1280:1536, 128:256]

    def forward(slot, tile, cond):
        s = spec[tile].astype(F32)
        turned = pltpu.roll(s, KF, 1)
        s2 = jnp.concatenate([s, s], 0)
        r2 = jnp.concatenate([turned, turned], 0)
        intensity = None
        for j in range(NK // 2):
            rows = slice(j * 128, (j + 1) * 128)
            mixed = (kre[cond, rows, :] * s2 + kim[cond, rows, :] * r2).astype(BF16)
            row_half = dot(mixed, t1[...]).astype(BF16)
            field = dot(t2[...], swap_pair(row_half))
            fields[slot, j] = field.astype(BF16)
            square = field * field
            square = square[:128] + square[128:]
            square = square[:, :128] + square[:, 128:]
            intensity = square if intensity is None else intensity + square
        return intensity

    def middle(intensity, tile, cond, live):
        hi = intensity.astype(BF16)
        lo = (intensity - hi.astype(F32)).astype(BF16)
        cols = dot(up2[...], jnp.concatenate([hi, lo], 0)) + dot(up_lo[...], hi)
        hi = cols.astype(BF16)
        lo = (cols - hi.astype(F32)).astype(BF16)
        full = dot(jnp.concatenate([hi, lo, hi], 1), upt3[...])
        tau = jnp.tanh((0.5 * STEEPNESS) * (full - thresholds[cond]))
        grad_int = 4.0 * (1.0 + tau - 2.0 * tgt[tile].astype(F32)) * (1.0 - tau * tau)
        down = dot(upt[...], grad_int.astype(BF16)).astype(BF16)
        coarse = dot(down, up[...])
        return jnp.where(live, coarse, 0.0)

    def backward(slot, coarse, tile, cond):
        wide = jnp.concatenate([coarse, coarse], 1)
        sum_re = None
        for j in range(NK // 2):
            rows = slice(j * 128, (j + 1) * 128)
            field = fields[slot, j].astype(F32)
            grad_field = jnp.concatenate([field[:128] * wide, field[128:] * wide], 0).astype(BF16)
            grad_half = dot(t2t[...], grad_field).astype(BF16)
            grad_mix = dot(swap_pair(grad_half), t1t[...])
            term_re = kre[cond, rows, :] * grad_mix
            term_im = kim[cond, rows, :] * grad_mix
            sum_re = term_re if sum_re is None else sum_re + term_re
            sum_im = term_im if j == 0 else sum_im + term_im
        total = sum_re[:KF] + sum_re[KF:] + pltpu.roll(sum_im[:KF] + sum_im[KF:], KF, 1)
        acc[tile] = acc[tile] + total

    def pick(test, a, b):
        return jnp.where(test, a, b).astype(jnp.int32)

    def unit_pair(i, carry):
        @pl.when(jnp.logical_not(heavy) & (i == 1))
        def _():
            target_copy.wait_recv()
            share_copy.wait_recv()

        outer = (i == 0) | (i == 3)
        first = pick(i == 0, 0, 2)
        tiles = [
            pick(heavy, i // 2, pick(outer, first, 4)),
            pick(heavy, i // 2, pick(outer, first + 1, 4)),
        ]
        low_cond = pick(heavy, (i % 2) * 2, pick(outer, 0, (i - 1) * 2))
        conds = [low_cond, pick(heavy, low_cond + 1, pick(outer, 0, low_cond + 1))]
        lives = [
            cond < counts[pick(tile == 4, partner, me), pick(tile == 4, 3, tile)]
            for tile, cond in zip(tiles, conds)
        ]
        sums = [forward(u, tiles[u], conds[u]) for u in range(2)]
        coarse = [middle(sums[u], tiles[u], conds[u], lives[u]) for u in range(2)]
        for u in range(2):
            backward(u, coarse[u], tiles[u], conds[u])

        @pl.when(jnp.logical_not(heavy) & (i == 2))
        def _():
            shared[...] = acc[4].astype(BF16)
            result_copy.start()

        return carry

    lax.fori_loop(0, jnp.where(heavy, 6, 4), unit_pair, jnp.int32(0))

    for k in range(3):
        gspec[1 + k // 2, 1 + k % 2] = acc[k].astype(BF16)

    @pl.when(jnp.logical_not(heavy))
    def _():
        gspec[2, 2] = acc[3].astype(BF16)
        result_copy.wait_send()

    @pl.when(heavy)
    def _():
        result_copy.wait_recv()
        share_copy.wait_send()
        target_copy.wait_send()

    for number, (dr, dc) in enumerate(WAYS):

        @pl.when(has(dr, dc))
        def _():
            spectrum_copy(number).wait_send()
            gradient_copy(number).start()

    for dr, dc in WAYS:

        @pl.when(jnp.logical_not(has(dr, dc)))
        def _():
            rows = 2 if dr == 0 else 1
            cols = 2 if dc == 0 else 1
            for i in range(rows):
                for j in range(cols):
                    a = {-1: 0, 0: 1 + i, 1: 3}[dr]
                    e = {-1: 0, 0: 1 + j, 1: 3}[dc]
                    gspec[a, e] = jnp.zeros((KF, 2 * KF), BF16)

    for number, (dr, dc) in enumerate(WAYS):

        @pl.when(has(dr, dc))
        def _():
            gradient_copy(number).wait_send()

        @pl.when(has(-dr, -dc))
        def _():
            gradient_copy(number).wait_recv()

    out[...] = gspec[...]


def adjoint_kernel(gspec, mask, edge, edge_t, levels_out, gradient_out, whole):
    r = pl.program_id(0)

    @pl.when(r == 0)
    def _():
        low = low_half((KF, 2 * KF))
        for a in range(4):
            for e in range(4):
                g = gspec[a, e].astype(F32)
                cols = slice(e * 128, (e + 1) * 128)
                whole[a * 128 : a * 128 + KF, cols] = jnp.where(low, g, -g).astype(BF16)
                whole[a * 128 + KF : (a + 1) * 128, cols] = (-pltpu.roll(g, KF, 1)).astype(BF16)

    start = pl.multiple_of(((r + 1) // 2) * 128, 128)
    halves = dot(edge[:, pl.ds(start, 256)], whole[pl.ds(start, 256), :]).astype(BF16)
    for cols, rows in (
        (slice(0, 128), slice(0, 256)),
        (slice(128, 384), slice(128, 384)),
        (slice(384, 512), slice(256, 512)),
    ):
        canvas = dot(halves[:, rows], edge_t[rows, cols])
        levels = mask[0, :, cols]
        transmit = jnp.tanh(0.5 * levels)
        gradient = canvas * (0.5 - 0.5 * transmit * transmit)
        gradient_out[0, :, cols] = gradient
        levels_out[0, :, cols] = levels - STEP_SIZE * gradient


def shards(mask_param, target, counts, kernels, weights, thresholds):
    edge = jnp.asarray(EDGE)
    edge_t = jnp.asarray(EDGE_T)
    unit = jnp.asarray(UNIT)
    any_space = pl.BlockSpec(memory_space=pl.ANY)
    smem = pl.BlockSpec(memory_space=pltpu.SMEM)
    block = (KF, 2 * KF)
    gspec = pl.pallas_call(
        gradient_kernel,
        out_shape=jax.ShapeDtypeStruct((4, 4) + block, BF16),
        in_specs=[smem] * 3 + [any_space] * 6,
        out_specs=pl.BlockSpec(memory_space=pltpu.VMEM),
        scratch_shapes=[
            pltpu.VMEM((512, 512), F32),
            pltpu.VMEM((512, 512), BF16),
            pltpu.VMEM((512, 512), BF16),
            pltpu.VMEM((4, 4) + block, BF16),
            pltpu.VMEM((4, 4) + block, BF16),
            pltpu.VMEM((5,) + block, BF16),
            pltpu.VMEM((5, TILE, TILE), BF16),
            pltpu.VMEM((CONDS, NK) + block, F32),
            pltpu.VMEM((CONDS, NK * KF, 2 * KF), F32),
            pltpu.VMEM((CONDS, NK * KF, 2 * KF), F32),
            pltpu.VMEM((2, NK // 2, 256, 256), BF16),
            pltpu.VMEM((5,) + block, F32),
            pltpu.VMEM((4, 4) + block, BF16),
            pltpu.VMEM(block, BF16),
            pltpu.VMEM((512, 512), BF16),
            pltpu.VMEM((512, 512), BF16),
            pltpu.VMEM(UNIT.shape, BF16),
            pltpu.SemaphoreType.DMA((9,)),
            pltpu.SemaphoreType.DMA((19,)),
            pltpu.SemaphoreType.DMA((19,)),
        ],
        compiler_params=pltpu.CompilerParams(
            collective_id=0, has_side_effects=True, vmem_limit_bytes=48 * 1024 * 1024
        ),
        name="gradient",
    )(counts, weights, thresholds, mask_param, target, kernels, edge, edge_t, unit)
    rows = pl.BlockSpec((1, 128, 512), lambda r: (0, r, 0))
    return pl.pallas_call(
        adjoint_kernel,
        grid=(4,),
        out_shape=(
            jax.ShapeDtypeStruct((1, 512, 512), F32),
            jax.ShapeDtypeStruct((1, 512, 512), F32),
        ),
        in_specs=[
            pl.BlockSpec((4, 4) + block, lambda r: (0, 0, 0, 0)),
            rows,
            pl.BlockSpec((128, 512), lambda r: (r, 0)),
            pl.BlockSpec((512, 512), lambda r: (0, 0)),
        ],
        out_specs=(rows, rows),
        scratch_shapes=[pltpu.VMEM((512, 512), BF16)],
        name="adjoint",
    )(gspec, mask_param, edge, edge_t)


def solution(mesh):
    placed = (P("tiles", None, None), P("tiles", None, None), P(), P(), P(), P())
    return jax.shard_map(
        shards,
        mesh=mesh,
        in_specs=placed,
        out_specs=(P("tiles", None, None), P("tiles", None, None)),
        check_vma=False,
    )
```

```python
import functools

import jax
import jax.numpy as jnp
import ml_dtypes
import numpy as np
from jax import lax
from jax.experimental import pallas as pl
from jax.experimental.pallas import tpu as pltpu
from jax.sharding import PartitionSpec as P

TILE = 256
HALO = 32
KF = 64
DEV_COLS = 8
PADDED = TILE + 2 * HALO
COARSE = 2 * KF
NK = 12
CONDS = 4
STEEPNESS = 8.0
STEP_SIZE = 0.25
SCALE = 1.0 / (PADDED * KF)

F32 = jnp.float32
BF16 = jnp.bfloat16
MESH = pl.DeviceIdType.MESH
WAYS = [(dr, dc) for dr in (-1, 0, 1) for dc in (-1, 0, 1) if (dr, dc) != (0, 0)]


def bf(values):
    return np.asarray(values, np.float32).astype(ml_dtypes.bfloat16)


def edge_table():
    freq = np.arange(KF) - KF // 2
    pixels = np.arange(PADDED)
    angles = 2.0 * np.pi * freq[:, None] * pixels[None, :] / PADDED
    forward = np.concatenate([np.cos(angles), np.sin(angles)], 0)
    table = np.zeros((2 * TILE, 4 * 2 * KF))
    for slot in range(4):
        first = (slot - 1) * TILE - HALO
        for pixel in range(2 * TILE):
            if 0 <= pixel - first < PADDED:
                table[pixel, slot * 2 * KF : (slot + 1) * 2 * KF] = forward[:, pixel - first]
    return bf(table)


def unit_tables():
    freq = np.arange(KF) - KF // 2
    angles = 2.0 * np.pi * np.arange(COARSE)[:, None] * freq[None, :] / COARSE
    cos_t, sin_t = np.cos(angles), np.sin(angles)
    t1 = np.block([[cos_t.T, sin_t.T], [-sin_t.T, cos_t.T]])
    t2 = np.block([[cos_t, -sin_t], [sin_t, cos_t]])
    shift = (np.arange(TILE) + HALO)[:, None] - PADDED / COARSE * np.arange(COARSE)[None, :]
    waves = np.arange(1, COARSE // 2)
    interp = (
        1.0 + 2.0 * np.cos(2.0 * np.pi * shift[:, :, None] * waves / PADDED).sum(-1)
    ) / COARSE
    up_hi = bf(interp)
    up_lo = bf(interp - up_hi.astype(np.float64))
    return np.concatenate(
        [
            bf(t1),
            bf(t2.T),
            up_hi.T,
            np.concatenate([up_hi, up_hi], 1),
            np.concatenate([up_hi.T, up_hi.T, up_lo.T], 0),
            np.concatenate([bf(t2), bf(t1.T)], 1),
            np.concatenate([up_lo, up_hi], 1),
        ],
        0,
    )


EDGE = edge_table()
EDGE_T = np.ascontiguousarray(EDGE.T)
UNIT = unit_tables()


def dot(a, b):
    return jnp.dot(a, b, preferred_element_type=F32)


def swap_pair(v):
    return jnp.concatenate(
        [
            jnp.concatenate([v[:64, :128], v[64:, :128]], 1),
            jnp.concatenate([v[:64, 128:], v[64:, 128:]], 1),
        ],
        0,
    )


def low_half(shape):
    return lax.broadcasted_iota(jnp.int32, shape, 1) < KF


def gradient_kernel(
    counts_in, weights_in, thresholds_in, mask, target, kernels, edge, edge_t, unit,
    out,
    levels, pixels, halves, part, got, spec, tgt, kraw, kre, kim, fields, acc, gspec, shared, edge_v, edge_tv, unit_v, counts, weights, thresholds,
    load_sem, send_sem, recv_sem,
):
    me = lax.axis_index("tiles")
    devices = lax.axis_size("tiles")
    quarter = devices // 4
    half = devices // 2
    my_col = me % DEV_COLS
    my_row = me // DEV_COLS
    grid_rows = devices // DEV_COLS
    heavy = me < half
    partner = me + (3 - 2 * (me // quarter)) * quarter

    def has(dr, dc):
        ok = (my_row + dr >= 0) & (my_row + dr < grid_rows)
        return ok & (my_col + dc >= 0) & (my_col + dc < DEV_COLS)

    def peer(dr, dc):
        return lax.rem(me + dr * DEV_COLS + dc + devices, devices)

    loads = [
        pltpu.make_async_copy(mask.at[0], levels, load_sem.at[0]),
        pltpu.make_async_copy(edge, edge_v, load_sem.at[1]),
        pltpu.make_async_copy(edge_t, edge_tv, load_sem.at[2]),
        pltpu.make_async_copy(kernels, kraw, load_sem.at[3]),
        pltpu.make_async_copy(unit, unit_v, load_sem.at[4]),
        pltpu.make_async_copy(counts_in, counts, load_sem.at[9]),
        pltpu.make_async_copy(thresholds_in, thresholds, load_sem.at[10]),
        pltpu.make_async_copy(weights_in, weights, load_sem.at[11]),
    ] + [
        pltpu.make_async_copy(
            target.at[0, pl.ds((k // 2) * TILE, TILE), pl.ds((k % 2) * TILE, TILE)],
            tgt.at[k],
            load_sem.at[5 + k],
        )
        for k in range(4)
    ]
    for load in loads:
        load.start()

    barrier = pltpu.get_barrier_semaphore()
    greeted = jnp.int32(1)
    for dr, dc in WAYS:
        greeted = greeted + has(dr, dc).astype(jnp.int32)

        @pl.when(has(dr, dc))
        def _():
            pl.semaphore_signal(barrier, inc=1, device_id=(peer(dr, dc),), device_id_type=MESH)

    pl.semaphore_signal(barrier, inc=1, device_id=(partner,), device_id_type=MESH)

    def remote(src, dst, number, to):
        return pltpu.make_async_remote_copy(
            src_ref=src,
            dst_ref=dst,
            send_sem=send_sem.at[number],
            recv_sem=recv_sem.at[number],
            device_id=(to,),
            device_id_type=MESH,
        )

    span = {-1: 0, 0: pl.ds(1, 2), 1: 3}
    back = {-1: 3, 0: pl.ds(1, 2), 1: 0}
    rim = {-1: 1, 0: pl.ds(1, 2), 1: 2}

    def spectrum_copy(number):
        dr, dc = WAYS[number]
        return remote(part.at[span[dr], span[dc]], got.at[back[dr], back[dc]], number, peer(dr, dc))

    def gradient_copy(number):
        dr, dc = WAYS[number]
        return remote(
            gspec.at[rim[dr], rim[dc]], gspec.at[back[dr], back[dc]], 8 + number, peer(dr, dc)
        )

    target_copy = remote(
        target.at[0, pl.ds(TILE, TILE), pl.ds(TILE, TILE)], tgt.at[4], 16, partner
    )
    share_copy = remote(spec.at[3], spec.at[4], 17, partner)
    result_copy = remote(shared, gspec.at[2, 2], 18, partner)

    for dr, dc in WAYS:

        @pl.when(jnp.logical_not(has(dr, dc)))
        def _():
            rows = 2 if dr == 0 else 1
            cols = 2 if dc == 0 else 1
            for i in range(rows):
                for j in range(cols):
                    a = {-1: 0, 0: 1 + i, 1: 3}[dr]
                    e = {-1: 0, 0: 1 + j, 1: 3}[dc]
                    got[a, e] = jnp.zeros((KF, 2 * KF), BF16)

    loads[0].wait()
    for r in range(4):
        rows = pl.ds(r * 128, 128)
        pixels[rows, :] = jnp.tanh(0.5 * levels[rows, :]).astype(BF16)

    pl.semaphore_wait(barrier, greeted)

    @pl.when(heavy)
    def _():
        target_copy.start()

    loads[1].wait()

    @pl.loop(0, 4)
    def _(r):
        rows = pl.ds(pl.multiple_of(r * 128, 128), 128)
        x = pixels[rows, :]
        halves[rows, 0:128] = dot(x[:, 0:128], edge_v[0:128, 0:128]).astype(BF16)
        halves[rows, 128:384] = dot(x, edge_v[:, 128:384]).astype(BF16)
        halves[rows, 384:512] = dot(x[:, 384:512], edge_v[384:512, 384:512]).astype(BF16)

    loads[2].wait()
    low = low_half((KF, 2 * KF))
    tall = {0: slice(0, 128), 1: slice(0, 384), 2: slice(128, 512), 3: slice(384, 512)}
    for a in (0, 3, 1, 2):
        prod = dot(edge_tv[a * 128 : (a + 1) * 128, tall[a]], halves[tall[a], :])
        for e in range(4):
            top = prod[:KF, e * 128 : (e + 1) * 128]
            low_rows = pltpu.roll(prod[KF:, e * 128 : (e + 1) * 128], KF, 1)
            value = jnp.where(low, top - low_rows, -(top + low_rows))
            if a in (1, 2) and e in (1, 2):
                acc[(a - 1) * 2 + e - 1] = value
            else:
                part[a, e] = value.astype(BF16)

    for number, (dr, dc) in enumerate(WAYS):

        @pl.when(has(dr, dc))
        def _():
            spectrum_copy(number).start()

    loads[3].wait()
    loads[7].wait()

    @pl.loop(0, CONDS)
    def _(c):
        for n in range(NK):
            k = kraw[c, n]
            amount = jnp.sqrt(jnp.full((1, 2 * KF), weights[c, n], F32)) * SCALE
            k = k * amount
            turned = pltpu.roll(k, KF, 1)
            kre[c, n * KF : (n + 1) * KF, :] = jnp.where(low, k, turned)
            kim[c, n * KF : (n + 1) * KF, :] = jnp.where(low, -turned, k)

    for load in loads[4:7] + loads[8:]:
        load.wait()

    for number, (dr, dc) in enumerate(WAYS):

        @pl.when(has(-dr, -dc))
        def _():
            spectrum_copy(number).wait_recv()

    for a in (1, 0):
        for e in (1, 0):
            oa = 3 * a
            oe = 3 * e
            total = (
                acc[a * 2 + e]
                + got[1 + a, oe].astype(F32)
                + got[oa, 1 + e].astype(F32)
                + got[oa, oe].astype(F32)
            )
            spec[a * 2 + e] = total.astype(BF16)
            acc[a * 2 + e] = jnp.zeros((KF, 2 * KF), F32)

        if a == 1:

            @pl.when(heavy)
            def _():
                share_copy.start()

    acc[4] = jnp.zeros((KF, 2 * KF), F32)

    t1 = unit_v.at[0:128, :]
    t2t = unit_v.at[128:256, :]
    upt = unit_v.at[256:384, :]
    up2 = unit_v.at[384:640, :]
    upt3 = unit_v.at[640:1024, :]
    t2 = unit_v.at[1024:1280, 0:128]
    t1t = unit_v.at[1024:1280, 128:256]
    up_lo = unit_v.at[1280:1536, 0:128]
    up = unit_v.at[1280:1536, 128:256]

    def forward(slot, tile, cond):
        s = spec[tile].astype(F32)
        turned = pltpu.roll(s, KF, 1)
        s2 = jnp.concatenate([s, s], 0)
        r2 = jnp.concatenate([turned, turned], 0)
        intensity = None
        for j in range(NK // 2):
            rows = slice(j * 128, (j + 1) * 128)
            mixed = (kre[cond, rows, :] * s2 + kim[cond, rows, :] * r2).astype(BF16)
            row_half = dot(mixed, t1[...]).astype(BF16)
            field = dot(t2[...], swap_pair(row_half))
            fields[slot, j] = field.astype(BF16)
            square = field * field
            square = square[:128] + square[128:]
            square = square[:, :128] + square[:, 128:]
            intensity = square if intensity is None else intensity + square
        return intensity

    def middle(intensity, tile, cond, live):
        hi = intensity.astype(BF16)
        lo = (intensity - hi.astype(F32)).astype(BF16)
        cols = dot(up2[...], jnp.concatenate([hi, lo], 0)) + dot(up_lo[...], hi)
        hi = cols.astype(BF16)
        lo = (cols - hi.astype(F32)).astype(BF16)
        full = dot(jnp.concatenate([hi, lo, hi], 1), upt3[...])
        tau = jnp.tanh((0.5 * STEEPNESS) * (full - thresholds[cond]))
        grad_int = 4.0 * (1.0 + tau - 2.0 * tgt[tile].astype(F32)) * (1.0 - tau * tau)
        down = dot(upt[...], grad_int.astype(BF16)).astype(BF16)
        coarse = dot(down, up[...])
        return jnp.where(live, coarse, 0.0)

    def backward(slot, coarse, tile, cond):
        wide = jnp.concatenate([coarse, coarse], 1)
        sum_re = None
        for j in range(NK // 2):
            rows = slice(j * 128, (j + 1) * 128)
            field = fields[slot, j].astype(F32)
            grad_field = jnp.concatenate([field[:128] * wide, field[128:] * wide], 0).astype(BF16)
            grad_half = dot(t2t[...], grad_field).astype(BF16)
            grad_mix = dot(swap_pair(grad_half), t1t[...])
            term_re = kre[cond, rows, :] * grad_mix
            term_im = kim[cond, rows, :] * grad_mix
            sum_re = term_re if sum_re is None else sum_re + term_re
            sum_im = term_im if j == 0 else sum_im + term_im
        total = sum_re[:KF] + sum_re[KF:] + pltpu.roll(sum_im[:KF] + sum_im[KF:], KF, 1)
        acc[tile] = acc[tile] + total

    def pick(test, a, b):
        return jnp.where(test, a, b).astype(jnp.int32)

    def unit_pair(i, carry):
        @pl.when(jnp.logical_not(heavy) & (i == 1))
        def _():
            target_copy.wait_recv()
            share_copy.wait_recv()

        outer = (i == 0) | (i == 3)
        first = pick(i == 0, 0, 2)
        tiles = [
            pick(heavy, i // 2, pick(outer, first, 4)),
            pick(heavy, i // 2, pick(outer, first + 1, 4)),
        ]
        low_cond = pick(heavy, (i % 2) * 2, pick(outer, 0, (i - 1) * 2))
        conds = [low_cond, pick(heavy, low_cond + 1, pick(outer, 0, low_cond + 1))]
        lives = [
            cond < counts[pick(tile == 4, 3, tile), pick(tile == 4, partner, me)]
            for tile, cond in zip(tiles, conds)
        ]
        sums = [forward(u, tiles[u], conds[u]) for u in range(2)]
        coarse = [middle(sums[u], tiles[u], conds[u], lives[u]) for u in range(2)]
        for u in range(2):
            backward(u, coarse[u], tiles[u], conds[u])

        @pl.when(jnp.logical_not(heavy) & (i == 2))
        def _():
            shared[...] = acc[4].astype(BF16)
            result_copy.start()

        return carry

    lax.fori_loop(0, jnp.where(heavy, 6, 4), unit_pair, jnp.int32(0))

    for k in range(3):
        gspec[1 + k // 2, 1 + k % 2] = acc[k].astype(BF16)

    @pl.when(jnp.logical_not(heavy))
    def _():
        gspec[2, 2] = acc[3].astype(BF16)
        result_copy.wait_send()

    @pl.when(heavy)
    def _():
        result_copy.wait_recv()
        share_copy.wait_send()
        target_copy.wait_send()

    for number, (dr, dc) in enumerate(WAYS):

        @pl.when(has(dr, dc))
        def _():
            spectrum_copy(number).wait_send()
            gradient_copy(number).start()

    for dr, dc in WAYS:

        @pl.when(jnp.logical_not(has(dr, dc)))
        def _():
            rows = 2 if dr == 0 else 1
            cols = 2 if dc == 0 else 1
            for i in range(rows):
                for j in range(cols):
                    a = {-1: 0, 0: 1 + i, 1: 3}[dr]
                    e = {-1: 0, 0: 1 + j, 1: 3}[dc]
                    gspec[a, e] = jnp.zeros((KF, 2 * KF), BF16)

    for number, (dr, dc) in enumerate(WAYS):

        @pl.when(has(dr, dc))
        def _():
            gradient_copy(number).wait_send()

        @pl.when(has(-dr, -dc))
        def _():
            gradient_copy(number).wait_recv()

    out[...] = gspec[...]


def adjoint_kernel(gspec, mask, edge, edge_t, levels_out, gradient_out, whole):
    r = pl.program_id(0)

    @pl.when(r == 0)
    def _():
        low = low_half((KF, 2 * KF))
        for a in range(4):
            for e in range(4):
                g = gspec[a, e].astype(F32)
                cols = slice(e * 128, (e + 1) * 128)
                whole[a * 128 : a * 128 + KF, cols] = jnp.where(low, g, -g).astype(BF16)
                whole[a * 128 + KF : (a + 1) * 128, cols] = (-pltpu.roll(g, KF, 1)).astype(BF16)

    start = pl.multiple_of(((r + 1) // 2) * 128, 128)
    halves = dot(edge[:, pl.ds(start, 256)], whole[pl.ds(start, 256), :]).astype(BF16)
    for cols, rows in (
        (slice(0, 128), slice(0, 256)),
        (slice(128, 384), slice(128, 384)),
        (slice(384, 512), slice(256, 512)),
    ):
        canvas = dot(halves[:, rows], edge_t[rows, cols])
        levels = mask[0, :, cols]
        transmit = jnp.tanh(0.5 * levels)
        gradient = canvas * (0.5 - 0.5 * transmit * transmit)
        gradient_out[0, :, cols] = gradient
        levels_out[0, :, cols] = levels - STEP_SIZE * gradient


def shards(mask_param, target, counts, kernels, weights, thresholds):
    edge = jnp.asarray(EDGE)
    edge_t = jnp.asarray(EDGE_T)
    unit = jnp.asarray(UNIT)
    any_space = pl.BlockSpec(memory_space=pltpu.HBM)
    block = (KF, 2 * KF)
    gspec = pl.pallas_call(
        gradient_kernel,
        out_shape=jax.ShapeDtypeStruct((4, 4) + block, BF16),
        in_specs=[any_space] * 9,
        out_specs=pl.BlockSpec(memory_space=pltpu.VMEM),
        scratch_shapes=[
            pltpu.VMEM((512, 512), F32),
            pltpu.VMEM((512, 512), BF16),
            pltpu.VMEM((512, 512), BF16),
            pltpu.VMEM((4, 4) + block, BF16),
            pltpu.VMEM((4, 4) + block, BF16),
            pltpu.VMEM((5,) + block, BF16),
            pltpu.VMEM((5, TILE, TILE), BF16),
            pltpu.VMEM((CONDS, NK) + block, F32),
            pltpu.VMEM((CONDS, NK * KF, 2 * KF), F32),
            pltpu.VMEM((CONDS, NK * KF, 2 * KF), F32),
            pltpu.VMEM((2, NK // 2, 256, 256), BF16),
            pltpu.VMEM((5,) + block, F32),
            pltpu.VMEM((4, 4) + block, BF16),
            pltpu.VMEM(block, BF16),
            pltpu.VMEM((512, 512), BF16),
            pltpu.VMEM((512, 512), BF16),
            pltpu.VMEM(UNIT.shape, BF16),
            pltpu.SMEM((4, 128), jnp.int32),
            pltpu.SMEM((CONDS, NK), F32),
            pltpu.SMEM((CONDS,), F32),
            pltpu.SemaphoreType.DMA((12,)),
            pltpu.SemaphoreType.DMA((19,)),
            pltpu.SemaphoreType.DMA((19,)),
        ],
        compiler_params=pltpu.CompilerParams(
            collective_id=0, has_side_effects=True, vmem_limit_bytes=67043328
        ),
        name="gradient",
    )(counts.T, weights, thresholds, mask_param, target, kernels, edge, edge_t, unit)
    rows = pl.BlockSpec((1, 128, 512), lambda r: (0, r, 0))
    return pl.pallas_call(
        adjoint_kernel,
        grid=(4,),
        out_shape=(
            jax.ShapeDtypeStruct((1, 512, 512), F32),
            jax.ShapeDtypeStruct((1, 512, 512), F32),
        ),
        in_specs=[
            pl.BlockSpec((4, 4) + block, lambda r: (0, 0, 0, 0)),
            rows,
            pl.BlockSpec((128, 512), lambda r: (r, 0)),
            pl.BlockSpec((512, 512), lambda r: (0, 0)),
        ],
        out_specs=(rows, rows),
        scratch_shapes=[pltpu.VMEM((512, 512), BF16)],
        name="adjoint",
    )(gspec, mask_param, edge, edge_t)


def solution(mesh):
    placed = (P("tiles", None, None), P("tiles", None, None), P(), P(), P(), P())
    return jax.shard_map(
        shards,
        mesh=mesh,
        in_specs=placed,
        out_specs=(P("tiles", None, None), P("tiles", None, None)),
        check_vma=False,
    )
```

```python
import functools

import jax
import jax.numpy as jnp
import ml_dtypes
import numpy as np
from jax import lax
from jax.experimental import pallas as pl
from jax.experimental.pallas import tpu as pltpu
from jax.sharding import PartitionSpec as P

TILE = 256
HALO = 32
KF = 64
DEV_COLS = 8
PADDED = TILE + 2 * HALO
COARSE = 2 * KF
NK = 12
CONDS = 4
STEEPNESS = 8.0
STEP_SIZE = 0.25
SCALE = 1.0 / (PADDED * KF)

F32 = jnp.float32
BF16 = jnp.bfloat16
MESH = pl.DeviceIdType.MESH
WAYS = [(dr, dc) for dr in (-1, 0, 1) for dc in (-1, 0, 1) if (dr, dc) != (0, 0)]


def bf(values):
    return np.asarray(values, np.float32).astype(ml_dtypes.bfloat16)


def edge_table():
    freq = np.arange(KF) - KF // 2
    pixels = np.arange(PADDED)
    angles = 2.0 * np.pi * freq[:, None] * pixels[None, :] / PADDED
    forward = np.concatenate([np.cos(angles), np.sin(angles)], 0)
    table = np.zeros((2 * TILE, 4 * 2 * KF))
    for slot in range(4):
        first = (slot - 1) * TILE - HALO
        for pixel in range(2 * TILE):
            if 0 <= pixel - first < PADDED:
                table[pixel, slot * 2 * KF : (slot + 1) * 2 * KF] = forward[:, pixel - first]
    return bf(table)


def unit_tables():
    freq = np.arange(KF) - KF // 2
    angles = 2.0 * np.pi * np.arange(COARSE)[:, None] * freq[None, :] / COARSE
    cos_t, sin_t = np.cos(angles), np.sin(angles)
    t1 = np.block([[cos_t.T, sin_t.T], [-sin_t.T, cos_t.T]])
    t2 = np.block([[cos_t, -sin_t], [sin_t, cos_t]])
    shift = (np.arange(TILE) + HALO)[:, None] - PADDED / COARSE * np.arange(COARSE)[None, :]
    waves = np.arange(1, COARSE // 2)
    interp = (
        1.0 + 2.0 * np.cos(2.0 * np.pi * shift[:, :, None] * waves / PADDED).sum(-1)
    ) / COARSE
    up_hi = bf(interp)
    up_lo = bf(interp - up_hi.astype(np.float64))
    return np.concatenate(
        [
            bf(t1),
            bf(t2.T),
            up_hi.T,
            np.concatenate([up_hi, up_lo], 1),
            np.concatenate([up_hi.T, up_lo.T], 0),
            np.concatenate([bf(t2), bf(t1.T)], 1),
        ],
        0,
    )


EDGE = edge_table()
EDGE_T = np.ascontiguousarray(EDGE.T)
UNIT = unit_tables()


def dot(a, b):
    return jnp.dot(a, b, preferred_element_type=F32)


def swap_pair(v):
    return jnp.concatenate(
        [
            jnp.concatenate([v[:64, :128], v[64:, :128]], 1),
            jnp.concatenate([v[:64, 128:], v[64:, 128:]], 1),
        ],
        0,
    )


def low_half(shape):
    return lax.broadcasted_iota(jnp.int32, shape, 1) < KF


def gradient_kernel(
    counts_in, weights_in, thresholds_in, mask, target, kernels, edge, edge_t, unit,
    out,
    levels, pixels, halves, part, got, spec, tgt, kraw, kre, kim, row_halves, fields, acc, gspec, shared, edge_v, edge_tv, unit_v, counts, weights, thresholds,
    load_sem, send_sem, recv_sem,
):
    me = lax.axis_index("tiles")
    devices = lax.axis_size("tiles")
    quarter = devices // 4
    half = devices // 2
    my_col = me % DEV_COLS
    my_row = me // DEV_COLS
    grid_rows = devices // DEV_COLS
    heavy = me < half
    partner = me + (3 - 2 * (me // quarter)) * quarter

    def has(dr, dc):
        ok = (my_row + dr >= 0) & (my_row + dr < grid_rows)
        return ok & (my_col + dc >= 0) & (my_col + dc < DEV_COLS)

    def peer(dr, dc):
        return lax.rem(me + dr * DEV_COLS + dc + devices, devices)

    loads = [
        pltpu.make_async_copy(mask.at[0], levels, load_sem.at[0]),
        pltpu.make_async_copy(edge, edge_v, load_sem.at[1]),
        pltpu.make_async_copy(edge_t, edge_tv, load_sem.at[2]),
        pltpu.make_async_copy(kernels, kraw, load_sem.at[3]),
        pltpu.make_async_copy(unit, unit_v, load_sem.at[4]),
        pltpu.make_async_copy(counts_in, counts, load_sem.at[9]),
        pltpu.make_async_copy(thresholds_in, thresholds, load_sem.at[10]),
        pltpu.make_async_copy(weights_in, weights, load_sem.at[11]),
    ] + [
        pltpu.make_async_copy(
            target.at[0, pl.ds((k // 2) * TILE, TILE), pl.ds((k % 2) * TILE, TILE)],
            tgt.at[k],
            load_sem.at[5 + k],
        )
        for k in range(4)
    ]
    for load in loads:
        load.start()

    barrier = pltpu.get_barrier_semaphore()
    greeted = jnp.int32(1)
    for dr, dc in WAYS:
        greeted = greeted + has(dr, dc).astype(jnp.int32)

        @pl.when(has(dr, dc))
        def _():
            pl.semaphore_signal(barrier, inc=1, device_id=(peer(dr, dc),), device_id_type=MESH)

    pl.semaphore_signal(barrier, inc=1, device_id=(partner,), device_id_type=MESH)

    def remote(src, dst, number, to):
        return pltpu.make_async_remote_copy(
            src_ref=src,
            dst_ref=dst,
            send_sem=send_sem.at[number],
            recv_sem=recv_sem.at[number],
            device_id=(to,),
            device_id_type=MESH,
        )

    span = {-1: 0, 0: pl.ds(1, 2), 1: 3}
    back = {-1: 3, 0: pl.ds(1, 2), 1: 0}
    rim = {-1: 1, 0: pl.ds(1, 2), 1: 2}

    def spectrum_copy(number):
        dr, dc = WAYS[number]
        return remote(part.at[span[dr], span[dc]], got.at[back[dr], back[dc]], number, peer(dr, dc))

    def gradient_copy(number):
        dr, dc = WAYS[number]
        return remote(
            gspec.at[rim[dr], rim[dc]], gspec.at[back[dr], back[dc]], 8 + number, peer(dr, dc)
        )

    target_copy = remote(
        target.at[0, pl.ds(TILE, TILE), pl.ds(TILE, TILE)], tgt.at[4], 16, partner
    )
    share_copy = remote(spec.at[3], spec.at[4], 17, partner)
    result_copy = remote(shared, gspec.at[2, 2], 18, partner)

    for dr, dc in WAYS:

        @pl.when(jnp.logical_not(has(dr, dc)))
        def _():
            rows = 2 if dr == 0 else 1
            cols = 2 if dc == 0 else 1
            for i in range(rows):
                for j in range(cols):
                    a = {-1: 0, 0: 1 + i, 1: 3}[dr]
                    e = {-1: 0, 0: 1 + j, 1: 3}[dc]
                    got[a, e] = jnp.zeros((KF, 2 * KF), BF16)

    loads[0].wait()
    for r in range(4):
        rows = pl.ds(r * 128, 128)
        pixels[rows, :] = jnp.tanh(0.5 * levels[rows, :]).astype(BF16)

    pl.semaphore_wait(barrier, greeted)

    @pl.when(heavy)
    def _():
        target_copy.start()

    loads[1].wait()

    @pl.loop(0, 4)
    def _(r):
        rows = pl.ds(pl.multiple_of(r * 128, 128), 128)
        x = pixels[rows, :]
        halves[rows, 0:128] = dot(x[:, 0:128], edge_v[0:128, 0:128]).astype(BF16)
        halves[rows, 128:384] = dot(x, edge_v[:, 128:384]).astype(BF16)
        halves[rows, 384:512] = dot(x[:, 384:512], edge_v[384:512, 384:512]).astype(BF16)

    loads[2].wait()
    low = low_half((KF, 2 * KF))
    tall = {0: slice(0, 128), 1: slice(0, 384), 2: slice(128, 512), 3: slice(384, 512)}
    for a in (0, 3, 1, 2):
        prod = dot(edge_tv[a * 128 : (a + 1) * 128, tall[a]], halves[tall[a], :])
        for e in range(4):
            top = prod[:KF, e * 128 : (e + 1) * 128]
            low_rows = pltpu.roll(prod[KF:, e * 128 : (e + 1) * 128], KF, 1)
            value = jnp.where(low, top - low_rows, -(top + low_rows))
            if a in (1, 2) and e in (1, 2):
                acc[(a - 1) * 2 + e - 1] = value
            else:
                part[a, e] = value.astype(BF16)

    for number, (dr, dc) in enumerate(WAYS):

        @pl.when(has(dr, dc))
        def _():
            spectrum_copy(number).start()

    loads[3].wait()
    loads[7].wait()

    @pl.loop(0, CONDS)
    def _(c):
        for n in range(NK):
            k = kraw[c, n]
            amount = jnp.sqrt(jnp.full((1, 2 * KF), weights[c, n], F32)) * SCALE
            k = k * amount
            turned = pltpu.roll(k, KF, 1)
            kre[c, n * KF : (n + 1) * KF, :] = jnp.where(low, k, turned)
            kim[c, n * KF : (n + 1) * KF, :] = jnp.where(low, -turned, k)

    for load in loads[4:7] + loads[8:]:
        load.wait()

    for number, (dr, dc) in enumerate(WAYS):

        @pl.when(has(-dr, -dc))
        def _():
            spectrum_copy(number).wait_recv()

    for a in (1, 0):
        for e in (1, 0):
            oa = 3 * a
            oe = 3 * e
            total = (
                acc[a * 2 + e]
                + got[1 + a, oe].astype(F32)
                + got[oa, 1 + e].astype(F32)
                + got[oa, oe].astype(F32)
            )
            spec[a * 2 + e] = total.astype(BF16)
            acc[a * 2 + e] = jnp.zeros((KF, 2 * KF), F32)

        if a == 1:

            @pl.when(heavy)
            def _():
                share_copy.start()

    acc[4] = jnp.zeros((KF, 2 * KF), F32)

    t1 = unit_v.at[0:128, :]
    t2t = unit_v.at[128:256, :]
    upt = unit_v.at[256:384, :]
    up2 = unit_v.at[384:640, :]
    upt2 = unit_v.at[640:896, :]
    t2 = unit_v.at[896:1152, 0:128]
    t1t = unit_v.at[896:1152, 128:256]
    up = unit_v.at[384:640, 0:128]

    def mix(slot, tile, cond):
        s = spec[tile].astype(F32)
        turned = pltpu.roll(s, KF, 1)
        s2 = jnp.concatenate([s, s], 0)
        r2 = jnp.concatenate([turned, turned], 0)
        for j in range(NK // 2):
            rows = slice(j * 128, (j + 1) * 128)
            mixed = (kre[cond, rows, :] * s2 + kim[cond, rows, :] * r2).astype(BF16)
            row_halves[slot, j] = swap_pair(dot(mixed, t1[...]).astype(BF16))

    def field(slot, j, intensity):
        value = dot(t2[...], row_halves[slot, j])
        fields[slot, j] = value.astype(BF16)
        square = value * value
        square = square[:128] + square[128:]
        square = square[:, :128] + square[:, 128:]
        return square if intensity is None else intensity + square

    def interpolate_rows(intensity):
        hi = intensity.astype(BF16)
        return dot(up2[...], jnp.concatenate([hi, hi], 0))

    def resist_gradient(cols, tile, cond):
        hi = cols.astype(BF16)
        full = dot(jnp.concatenate([hi, hi], 1), upt2[...])
        tau = jnp.tanh((0.5 * STEEPNESS) * (full - thresholds[cond]))
        grad_int = 4.0 * (1.0 + tau - 2.0 * tgt[tile].astype(F32)) * (1.0 - tau * tau)
        return grad_int.astype(BF16)

    def coarse_rows(grad_int):
        return dot(upt[...], grad_int).astype(BF16)

    def coarse_gradient(down, live):
        return jnp.where(live, dot(down, up[...]), 0.0).astype(BF16)

    def grad_halves(slot, j, coarse):
        wide = jnp.concatenate([coarse, coarse], 1)
        value = fields[slot, j]
        grad_field = jnp.concatenate([value[:128] * wide, value[128:] * wide], 0)
        row_halves[slot, j] = swap_pair(dot(t2t[...], grad_field).astype(BF16))

    def gather(slot, tile, cond):
        sum_re = None
        for j in range(NK // 2):
            rows = slice(j * 128, (j + 1) * 128)
            grad_mix = dot(row_halves[slot, j], t1t[...])
            term_re = kre[cond, rows, :] * grad_mix
            term_im = kim[cond, rows, :] * grad_mix
            sum_re = term_re if j == 0 else sum_re + term_re
            sum_im = term_im if j == 0 else sum_im + term_im
        total = sum_re[:KF] + sum_re[KF:] + pltpu.roll(sum_im[:KF] + sum_im[KF:], KF, 1)
        acc[tile] = acc[tile] + total

    def pick(test, a, b):
        return jnp.where(test, a, b).astype(jnp.int32)

    def unit_pair(i, carry):
        @pl.when(jnp.logical_not(heavy) & (i == 1))
        def _():
            target_copy.wait_recv()
            share_copy.wait_recv()

        outer = (i == 0) | (i == 3)
        first = pick(i == 0, 0, 2)
        tiles = [
            pick(heavy, i // 2, pick(outer, first, 4)),
            pick(heavy, i // 2, pick(outer, first + 1, 4)),
        ]
        low_cond = pick(heavy, (i % 2) * 2, pick(outer, 0, (i - 1) * 2))
        conds = [low_cond, pick(heavy, low_cond + 1, pick(outer, 0, low_cond + 1))]
        lives = [
            cond < counts[pick(tile == 4, 3, tile), pick(tile == 4, partner, me)]
            for tile, cond in zip(tiles, conds)
        ]
        for u in range(2):
            mix(u, tiles[u], conds[u])
        bright = [None, None]
        for j in range(6):
            bright[0] = field(0, j, bright[0])
        for j in range(2):
            bright[1] = field(1, j, bright[1])
        cols = interpolate_rows(bright[0])
        bright[1] = field(1, 2, bright[1])
        grad_int = resist_gradient(cols, tiles[0], conds[0])
        bright[1] = field(1, 3, bright[1])
        bright[1] = field(1, 4, bright[1])
        down = coarse_rows(grad_int)
        bright[1] = field(1, 5, bright[1])
        coarse = coarse_gradient(down, lives[0])
        cols = interpolate_rows(bright[1])
        for j in range(2):
            grad_halves(0, j, coarse)
        grad_int = resist_gradient(cols, tiles[1], conds[1])
        for j in range(2, 4):
            grad_halves(0, j, coarse)
        down = coarse_rows(grad_int)
        for j in range(4, 6):
            grad_halves(0, j, coarse)
        coarse = coarse_gradient(down, lives[1])
        gather(0, tiles[0], conds[0])
        for j in range(6):
            grad_halves(1, j, coarse)
        gather(1, tiles[1], conds[1])

        @pl.when(jnp.logical_not(heavy) & (i == 2))
        def _():
            shared[...] = acc[4].astype(BF16)
            result_copy.start()

        return carry

    lax.fori_loop(0, jnp.where(heavy, 6, 4), unit_pair, jnp.int32(0))

    for k in range(3):
        gspec[1 + k // 2, 1 + k % 2] = acc[k].astype(BF16)

    @pl.when(jnp.logical_not(heavy))
    def _():
        gspec[2, 2] = acc[3].astype(BF16)
        result_copy.wait_send()

    @pl.when(heavy)
    def _():
        result_copy.wait_recv()
        share_copy.wait_send()
        target_copy.wait_send()

    for number, (dr, dc) in enumerate(WAYS):

        @pl.when(has(dr, dc))
        def _():
            spectrum_copy(number).wait_send()
            gradient_copy(number).start()

    for dr, dc in WAYS:

        @pl.when(jnp.logical_not(has(dr, dc)))
        def _():
            rows = 2 if dr == 0 else 1
            cols = 2 if dc == 0 else 1
            for i in range(rows):
                for j in range(cols):
                    a = {-1: 0, 0: 1 + i, 1: 3}[dr]
                    e = {-1: 0, 0: 1 + j, 1: 3}[dc]
                    gspec[a, e] = jnp.zeros((KF, 2 * KF), BF16)

    for number, (dr, dc) in enumerate(WAYS):

        @pl.when(has(dr, dc))
        def _():
            gradient_copy(number).wait_send()

        @pl.when(has(-dr, -dc))
        def _():
            gradient_copy(number).wait_recv()

    out[...] = gspec[...]


def adjoint_kernel(gspec, mask, edge, edge_t, levels_out, gradient_out, whole):
    r = pl.program_id(0)

    @pl.when(r == 0)
    def _():
        low = low_half((KF, 2 * KF))
        for a in range(4):
            for e in range(4):
                g = gspec[a, e].astype(F32)
                cols = slice(e * 128, (e + 1) * 128)
                whole[a * 128 : a * 128 + KF, cols] = jnp.where(low, g, -g).astype(BF16)
                whole[a * 128 + KF : (a + 1) * 128, cols] = (-pltpu.roll(g, KF, 1)).astype(BF16)

    start = pl.multiple_of(((r + 1) // 2) * 128, 128)
    halves = dot(edge[:, pl.ds(start, 256)], whole[pl.ds(start, 256), :]).astype(BF16)
    for cols, rows in (
        (slice(0, 128), slice(0, 256)),
        (slice(128, 384), slice(128, 384)),
        (slice(384, 512), slice(256, 512)),
    ):
        canvas = dot(halves[:, rows], edge_t[rows, cols])
        levels = mask[0, :, cols]
        transmit = jnp.tanh(0.5 * levels)
        gradient = canvas * (0.5 - 0.5 * transmit * transmit)
        gradient_out[0, :, cols] = gradient
        levels_out[0, :, cols] = levels - STEP_SIZE * gradient


def shards(mask_param, target, counts, kernels, weights, thresholds):
    edge = jnp.asarray(EDGE)
    edge_t = jnp.asarray(EDGE_T)
    unit = jnp.asarray(UNIT)
    any_space = pl.BlockSpec(memory_space=pltpu.HBM)
    block = (KF, 2 * KF)
    gspec = pl.pallas_call(
        gradient_kernel,
        out_shape=jax.ShapeDtypeStruct((4, 4) + block, BF16),
        in_specs=[any_space] * 9,
        out_specs=pl.BlockSpec(memory_space=pltpu.VMEM),
        scratch_shapes=[
            pltpu.VMEM((512, 512), F32),
            pltpu.VMEM((512, 512), BF16),
            pltpu.VMEM((512, 512), BF16),
            pltpu.VMEM((4, 4) + block, BF16),
            pltpu.VMEM((4, 4) + block, BF16),
            pltpu.VMEM((5,) + block, BF16),
            pltpu.VMEM((5, TILE, TILE), BF16),
            pltpu.VMEM((CONDS, NK) + block, F32),
            pltpu.VMEM((CONDS, NK * KF, 2 * KF), F32),
            pltpu.VMEM((CONDS, NK * KF, 2 * KF), F32),
            pltpu.VMEM((2, NK // 2, 128, 256), BF16),
            pltpu.VMEM((2, NK // 2, 256, 256), BF16),
            pltpu.VMEM((5,) + block, F32),
            pltpu.VMEM((4, 4) + block, BF16),
            pltpu.VMEM(block, BF16),
            pltpu.VMEM((512, 512), BF16),
            pltpu.VMEM((512, 512), BF16),
            pltpu.VMEM(UNIT.shape, BF16),
            pltpu.SMEM((4, 128), jnp.int32),
            pltpu.SMEM((CONDS, NK), F32),
            pltpu.SMEM((CONDS,), F32),
            pltpu.SemaphoreType.DMA((12,)),
            pltpu.SemaphoreType.DMA((19,)),
            pltpu.SemaphoreType.DMA((19,)),
        ],
        compiler_params=pltpu.CompilerParams(
            collective_id=0, has_side_effects=True, vmem_limit_bytes=67043328
        ),
        name="gradient",
    )(counts.T, weights, thresholds, mask_param, target, kernels, edge, edge_t, unit)
    rows = pl.BlockSpec((1, 128, 512), lambda r: (0, r, 0))
    return pl.pallas_call(
        adjoint_kernel,
        grid=(4,),
        out_shape=(
            jax.ShapeDtypeStruct((1, 512, 512), F32),
            jax.ShapeDtypeStruct((1, 512, 512), F32),
        ),
        in_specs=[
            pl.BlockSpec((4, 4) + block, lambda r: (0, 0, 0, 0)),
            rows,
            pl.BlockSpec((128, 512), lambda r: (r, 0)),
            pl.BlockSpec((512, 512), lambda r: (0, 0)),
        ],
        out_specs=(rows, rows),
        scratch_shapes=[pltpu.VMEM((512, 512), BF16)],
        name="adjoint",
    )(gspec, mask_param, edge, edge_t)


def solution(mesh):
    placed = (P("tiles", None, None), P("tiles", None, None), P(), P(), P(), P())
    return jax.shard_map(
        shards,
        mesh=mesh,
        in_specs=placed,
        out_specs=(P("tiles", None, None), P("tiles", None, None)),
        check_vma=False,
    )
```

```python
import functools

import jax
import jax.numpy as jnp
import ml_dtypes
import numpy as np
from jax import lax
from jax.experimental import pallas as pl
from jax.experimental.pallas import tpu as pltpu
from jax.sharding import PartitionSpec as P

TILE = 256
HALO = 32
KF = 64
DEV_COLS = 8
PADDED = TILE + 2 * HALO
COARSE = 2 * KF
NK = 12
CONDS = 4
UNITS = 4
STEEPNESS = 8.0
STEP_SIZE = 0.25
SCALE = 1.0 / (PADDED * KF)

F32 = jnp.float32
BF16 = jnp.bfloat16
MESH = pl.DeviceIdType.MESH
WAYS = [(dr, dc) for dr in (-1, 0, 1) for dc in (-1, 0, 1) if (dr, dc) != (0, 0)]


def bf(values):
    return np.asarray(values, np.float32).astype(ml_dtypes.bfloat16)


def edge_table():
    freq = np.arange(KF) - KF // 2
    pixels = np.arange(PADDED)
    angles = 2.0 * np.pi * freq[:, None] * pixels[None, :] / PADDED
    forward = np.concatenate([np.cos(angles), np.sin(angles)], 0)
    table = np.zeros((2 * TILE, 4 * 2 * KF))
    for slot in range(4):
        first = (slot - 1) * TILE - HALO
        for pixel in range(2 * TILE):
            if 0 <= pixel - first < PADDED:
                table[pixel, slot * 2 * KF : (slot + 1) * 2 * KF] = forward[:, pixel - first]
    return bf(table)


def unit_tables():
    freq = np.arange(KF) - KF // 2
    angles = 2.0 * np.pi * np.arange(COARSE)[:, None] * freq[None, :] / COARSE
    cos_t, sin_t = np.cos(angles), np.sin(angles)
    t1 = np.block([[cos_t.T, sin_t.T], [-sin_t.T, cos_t.T]])
    t2 = np.block([[cos_t, -sin_t], [sin_t, cos_t]])
    shift = (np.arange(TILE) + HALO)[:, None] - PADDED / COARSE * np.arange(COARSE)[None, :]
    waves = np.arange(1, COARSE // 2)
    interp = (
        1.0 + 2.0 * np.cos(2.0 * np.pi * shift[:, :, None] * waves / PADDED).sum(-1)
    ) / COARSE
    up_hi = bf(interp)
    up_lo = bf(interp - up_hi.astype(np.float64))
    return np.concatenate(
        [
            bf(t1),
            bf(t2.T),
            up_hi.T,
            np.concatenate([up_hi, up_lo], 1),
            np.concatenate([up_hi.T, up_lo.T], 0),
            np.concatenate([bf(t2), bf(t1.T)], 1),
        ],
        0,
    )


EDGE = edge_table()
EDGE_T = np.ascontiguousarray(EDGE.T)
UNIT = unit_tables()


def dot(a, b):
    return jnp.dot(a, b, preferred_element_type=F32)


def swap_pair(v):
    return jnp.concatenate(
        [
            jnp.concatenate([v[:64, :128], v[64:, :128]], 1),
            jnp.concatenate([v[:64, 128:], v[64:, 128:]], 1),
        ],
        0,
    )


def low_half(shape):
    return lax.broadcasted_iota(jnp.int32, shape, 1) < KF


def gradient_kernel(
    counts_in, weights_in, thresholds_in, mask, target, kernels, edge, edge_t, unit,
    out,
    levels, pixels, halves, part, got, spec, tgt, kraw, kre, kim, row_halves, fields, acc, gspec, shared, edge_v, edge_tv, unit_v, counts, weights, thresholds,
    load_sem, send_sem, recv_sem,
):
    me = lax.axis_index("tiles")
    devices = lax.axis_size("tiles")
    quarter = devices // 4
    half = devices // 2
    my_col = me % DEV_COLS
    my_row = me // DEV_COLS
    grid_rows = devices // DEV_COLS
    heavy = me < half
    partner = me + (3 - 2 * (me // quarter)) * quarter

    def has(dr, dc):
        ok = (my_row + dr >= 0) & (my_row + dr < grid_rows)
        return ok & (my_col + dc >= 0) & (my_col + dc < DEV_COLS)

    def peer(dr, dc):
        return lax.rem(me + dr * DEV_COLS + dc + devices, devices)

    loads = [
        pltpu.make_async_copy(mask.at[0], levels, load_sem.at[0]),
        pltpu.make_async_copy(edge, edge_v, load_sem.at[1]),
        pltpu.make_async_copy(edge_t, edge_tv, load_sem.at[2]),
        pltpu.make_async_copy(kernels, kraw, load_sem.at[3]),
        pltpu.make_async_copy(unit, unit_v, load_sem.at[4]),
        pltpu.make_async_copy(counts_in, counts, load_sem.at[9]),
        pltpu.make_async_copy(thresholds_in, thresholds, load_sem.at[10]),
        pltpu.make_async_copy(weights_in, weights, load_sem.at[11]),
    ] + [
        pltpu.make_async_copy(
            target.at[0, pl.ds((k // 2) * TILE, TILE), pl.ds((k % 2) * TILE, TILE)],
            tgt.at[k],
            load_sem.at[5 + k],
        )
        for k in range(4)
    ]
    for load in loads:
        load.start()

    barrier = pltpu.get_barrier_semaphore()
    greeted = jnp.int32(1)
    for dr, dc in WAYS:
        greeted = greeted + has(dr, dc).astype(jnp.int32)

        @pl.when(has(dr, dc))
        def _():
            pl.semaphore_signal(barrier, inc=1, device_id=(peer(dr, dc),), device_id_type=MESH)

    pl.semaphore_signal(barrier, inc=1, device_id=(partner,), device_id_type=MESH)

    def remote(src, dst, number, to):
        return pltpu.make_async_remote_copy(
            src_ref=src,
            dst_ref=dst,
            send_sem=send_sem.at[number],
            recv_sem=recv_sem.at[number],
            device_id=(to,),
            device_id_type=MESH,
        )

    span = {-1: 0, 0: pl.ds(1, 2), 1: 3}
    back = {-1: 3, 0: pl.ds(1, 2), 1: 0}
    rim = {-1: 1, 0: pl.ds(1, 2), 1: 2}

    def spectrum_copy(number):
        dr, dc = WAYS[number]
        return remote(part.at[span[dr], span[dc]], got.at[back[dr], back[dc]], number, peer(dr, dc))

    def gradient_copy(number):
        dr, dc = WAYS[number]
        return remote(
            gspec.at[rim[dr], rim[dc]], gspec.at[back[dr], back[dc]], 8 + number, peer(dr, dc)
        )

    target_copy = remote(
        target.at[0, pl.ds(TILE, TILE), pl.ds(TILE, TILE)], tgt.at[4], 16, partner
    )
    share_copy = remote(spec.at[3], spec.at[4], 17, partner)
    result_copy = remote(shared, gspec.at[2, 2], 18, partner)

    for dr, dc in WAYS:

        @pl.when(jnp.logical_not(has(dr, dc)))
        def _():
            rows = 2 if dr == 0 else 1
            cols = 2 if dc == 0 else 1
            for i in range(rows):
                for j in range(cols):
                    a = {-1: 0, 0: 1 + i, 1: 3}[dr]
                    e = {-1: 0, 0: 1 + j, 1: 3}[dc]
                    got[a, e] = jnp.zeros((KF, 2 * KF), BF16)

    loads[0].wait()
    for r in range(4):
        rows = pl.ds(r * 128, 128)
        pixels[rows, :] = jnp.tanh(0.5 * levels[rows, :]).astype(BF16)

    pl.semaphore_wait(barrier, greeted)

    @pl.when(heavy)
    def _():
        target_copy.start()

    loads[1].wait()

    @pl.loop(0, 4)
    def _(r):
        rows = pl.ds(pl.multiple_of(r * 128, 128), 128)
        x = pixels[rows, :]
        halves[rows, 0:128] = dot(x[:, 0:128], edge_v[0:128, 0:128]).astype(BF16)
        halves[rows, 128:384] = dot(x, edge_v[:, 128:384]).astype(BF16)
        halves[rows, 384:512] = dot(x[:, 384:512], edge_v[384:512, 384:512]).astype(BF16)

    loads[2].wait()
    low = low_half((KF, 2 * KF))
    tall = {0: slice(0, 128), 1: slice(0, 384), 2: slice(128, 512), 3: slice(384, 512)}
    for a in (0, 3, 1, 2):
        prod = dot(edge_tv[a * 128 : (a + 1) * 128, tall[a]], halves[tall[a], :])
        for e in range(4):
            top = prod[:KF, e * 128 : (e + 1) * 128]
            low_rows = pltpu.roll(prod[KF:, e * 128 : (e + 1) * 128], KF, 1)
            value = jnp.where(low, top - low_rows, -(top + low_rows))
            if a in (1, 2) and e in (1, 2):
                acc[(a - 1) * 2 + e - 1] = value
            else:
                part[a, e] = value.astype(BF16)

    for number, (dr, dc) in enumerate(WAYS):

        @pl.when(has(dr, dc))
        def _():
            spectrum_copy(number).start()

    loads[3].wait()
    loads[7].wait()

    @pl.loop(0, CONDS)
    def _(c):
        for n in range(NK):
            k = kraw[c, n]
            amount = jnp.sqrt(jnp.full((1, 2 * KF), weights[c, n], F32)) * SCALE
            k = k * amount
            turned = pltpu.roll(k, KF, 1)
            kre[c, n * KF : (n + 1) * KF, :] = jnp.where(low, k, turned)
            kim[c, n * KF : (n + 1) * KF, :] = jnp.where(low, -turned, k)

    for load in loads[4:7] + loads[8:]:
        load.wait()

    for number, (dr, dc) in enumerate(WAYS):

        @pl.when(has(-dr, -dc))
        def _():
            spectrum_copy(number).wait_recv()

    for a in (1, 0):
        for e in (1, 0):
            oa = 3 * a
            oe = 3 * e
            total = (
                acc[a * 2 + e]
                + got[1 + a, oe].astype(F32)
                + got[oa, 1 + e].astype(F32)
                + got[oa, oe].astype(F32)
            )
            spec[a * 2 + e] = total.astype(BF16)
            acc[a * 2 + e] = jnp.zeros((KF, 2 * KF), F32)

        if a == 1:

            @pl.when(heavy)
            def _():
                share_copy.start()

    acc[4] = jnp.zeros((KF, 2 * KF), F32)

    t1 = unit_v.at[0:128, :]
    t2t = unit_v.at[128:256, :]
    upt = unit_v.at[256:384, :]
    up2 = unit_v.at[384:640, :]
    upt2 = unit_v.at[640:896, :]
    t2 = unit_v.at[896:1152, 0:128]
    t1t = unit_v.at[896:1152, 128:256]
    up = unit_v.at[384:640, 0:128]

    def mix(slot, tile, cond):
        s = spec[tile].astype(F32)
        turned = pltpu.roll(s, KF, 1)
        s2 = jnp.concatenate([s, s], 0)
        r2 = jnp.concatenate([turned, turned], 0)
        for j in range(NK // 2):
            rows = slice(j * 128, (j + 1) * 128)
            mixed = (kre[cond, rows, :] * s2 + kim[cond, rows, :] * r2).astype(BF16)
            row_halves[slot, j] = swap_pair(dot(mixed, t1[...]).astype(BF16))

    def field(slot, j, intensity):
        value = dot(t2[...], row_halves[slot, j])
        fields[slot, j] = value.astype(BF16)
        square = value * value
        square = square[:128] + square[128:]
        square = square[:, :128] + square[:, 128:]
        return square if intensity is None else intensity + square

    def interpolate_rows(intensity):
        hi = intensity.astype(BF16)
        return dot(up2[...], jnp.concatenate([hi, hi], 0))

    def resist_gradient(cols, tile, cond):
        hi = cols.astype(BF16)
        full = dot(jnp.concatenate([hi, hi], 1), upt2[...])
        tau = jnp.tanh((0.5 * STEEPNESS) * (full - thresholds[cond]))
        grad_int = 4.0 * (1.0 + tau - 2.0 * tgt[tile].astype(F32)) * (1.0 - tau * tau)
        return grad_int.astype(BF16)

    def coarse_rows(grad_int):
        return dot(upt[...], grad_int).astype(BF16)

    def coarse_gradient(down, live):
        return jnp.where(live, dot(down, up[...]), 0.0).astype(BF16)

    def grad_halves(slot, j, coarse):
        wide = jnp.concatenate([coarse, coarse], 1)
        value = fields[slot, j]
        grad_field = jnp.concatenate([value[:128] * wide, value[128:] * wide], 0)
        row_halves[slot, j] = swap_pair(dot(t2t[...], grad_field).astype(BF16))

    def gather(slot, tile, cond):
        sum_re = None
        for j in range(NK // 2):
            rows = slice(j * 128, (j + 1) * 128)
            grad_mix = dot(row_halves[slot, j], t1t[...])
            term_re = kre[cond, rows, :] * grad_mix
            term_im = kim[cond, rows, :] * grad_mix
            sum_re = term_re if j == 0 else sum_re + term_re
            sum_im = term_im if j == 0 else sum_im + term_im
        total = sum_re[:KF] + sum_re[KF:] + pltpu.roll(sum_im[:KF] + sum_im[KF:], KF, 1)
        acc[tile] = acc[tile] + total

    def pick(test, a, b):
        return jnp.where(test, a, b).astype(jnp.int32)

    def unit_group(i, carry):
        @pl.when(jnp.logical_not(heavy) & (i == 1))
        def _():
            target_copy.wait_recv()
            share_copy.wait_recv()

        own = jnp.logical_not(heavy) & (i == 0)
        tile = pick(heavy, i, 4)
        tiles = [pick(own, u, tile) for u in range(UNITS)]
        conds = [pick(own, 0, u) for u in range(UNITS)]
        lives = [
            cond < counts[pick(tile == 4, 3, tile), pick(tile == 4, partner, me)]
            for tile, cond in zip(tiles, conds)
        ]
        args = list(zip(tiles, conds))
        bright = [None] * UNITS
        coarse = [None] * UNITS

        def fields_step(u, j):
            bright[u] = field(u, j, bright[u])

        def halves_step(u, j):
            grad_halves(u, j, coarse[u])

        def middle_between(u, steps):
            cols = interpolate_rows(bright[u])
            for step in steps[:2]:
                step()
            grad_int = resist_gradient(cols, *args[u])
            for step in steps[2:4]:
                step()
            down = coarse_rows(grad_int)
            for step in steps[4:]:
                step()
            coarse[u] = coarse_gradient(down, lives[u])

        for u in range(UNITS):
            mix(u, *args[u])
        for j in range(6):
            fields_step(0, j)
        for u in range(UNITS - 1):
            middle_between(u, [functools.partial(fields_step, u + 1, j) for j in range(6)])
        middle_between(UNITS - 1, [functools.partial(halves_step, 0, j) for j in range(6)])
        for u in range(1, UNITS):
            for j in range(6):
                halves_step(u, j)
            gather(u - 1, *args[u - 1])
        gather(UNITS - 1, *args[UNITS - 1])

        @pl.when(jnp.logical_not(heavy) & (i == 1))
        def _():
            shared[...] = acc[4].astype(BF16)
            result_copy.start()

        return carry

    lax.fori_loop(0, jnp.where(heavy, 3, 2), unit_group, jnp.int32(0))

    for k in range(3):
        gspec[1 + k // 2, 1 + k % 2] = acc[k].astype(BF16)

    @pl.when(jnp.logical_not(heavy))
    def _():
        gspec[2, 2] = acc[3].astype(BF16)
        result_copy.wait_send()

    @pl.when(heavy)
    def _():
        result_copy.wait_recv()
        share_copy.wait_send()
        target_copy.wait_send()

    for number, (dr, dc) in enumerate(WAYS):

        @pl.when(has(dr, dc))
        def _():
            spectrum_copy(number).wait_send()
            gradient_copy(number).start()

    for dr, dc in WAYS:

        @pl.when(jnp.logical_not(has(dr, dc)))
        def _():
            rows = 2 if dr == 0 else 1
            cols = 2 if dc == 0 else 1
            for i in range(rows):
                for j in range(cols):
                    a = {-1: 0, 0: 1 + i, 1: 3}[dr]
                    e = {-1: 0, 0: 1 + j, 1: 3}[dc]
                    gspec[a, e] = jnp.zeros((KF, 2 * KF), BF16)

    for number, (dr, dc) in enumerate(WAYS):

        @pl.when(has(dr, dc))
        def _():
            gradient_copy(number).wait_send()

        @pl.when(has(-dr, -dc))
        def _():
            gradient_copy(number).wait_recv()

    out[...] = gspec[...]


def adjoint_kernel(gspec, mask, edge, edge_t, levels_out, gradient_out, whole, levels, gradient, sem):
    low = low_half((KF, 2 * KF))

    def unfold(a):
        for e in range(4):
            g = gspec[a, e].astype(F32)
            cols = slice(e * 128, (e + 1) * 128)
            whole[a * 128 : a * 128 + KF, cols] = jnp.where(low, g, -g).astype(BF16)
            whole[a * 128 + KF : (a + 1) * 128, cols] = (-pltpu.roll(g, KF, 1)).astype(BF16)

    copies = []
    for r in range(4):
        for a in {0: (0, 1), 1: (2,), 2: (), 3: (3,)}[r]:
            unfold(a)
        rows = slice(r * 128, (r + 1) * 128)
        start = ((r + 1) // 2) * 128
        halves = dot(edge[rows, start : start + 256], whole[start : start + 256, :]).astype(BF16)
        for cols, tall in (
            (slice(0, 128), slice(0, 256)),
            (slice(128, 384), slice(128, 384)),
            (slice(384, 512), slice(256, 512)),
        ):
            canvas = dot(halves[:, tall], edge_t[tall, cols])
            before = mask[0, rows, cols]
            transmit = jnp.tanh(0.5 * before)
            grad = canvas * (0.5 - 0.5 * transmit * transmit)
            gradient[rows, cols] = grad
            levels[rows, cols] = before - STEP_SIZE * grad
        for k, (source, out) in enumerate(((gradient, gradient_out), (levels, levels_out))):
            copy = pltpu.make_async_copy(source.at[rows], out.at[0, rows], sem.at[k, r])
            copy.start()
            copies.append(copy)
    for copy in copies:
        copy.wait()


def shards(mask_param, target, counts, kernels, weights, thresholds):
    edge = jnp.asarray(EDGE)
    edge_t = jnp.asarray(EDGE_T)
    unit = jnp.asarray(UNIT)
    any_space = pl.BlockSpec(memory_space=pltpu.HBM)
    block = (KF, 2 * KF)
    gspec = pl.pallas_call(
        gradient_kernel,
        out_shape=jax.ShapeDtypeStruct((4, 4) + block, BF16),
        in_specs=[any_space] * 9,
        out_specs=pl.BlockSpec(memory_space=pltpu.VMEM),
        scratch_shapes=[
            pltpu.VMEM((512, 512), F32),
            pltpu.VMEM((512, 512), BF16),
            pltpu.VMEM((512, 512), BF16),
            pltpu.VMEM((4, 4) + block, BF16),
            pltpu.VMEM((4, 4) + block, BF16),
            pltpu.VMEM((5,) + block, BF16),
            pltpu.VMEM((5, TILE, TILE), BF16),
            pltpu.VMEM((CONDS, NK) + block, F32),
            pltpu.VMEM((CONDS, NK * KF, 2 * KF), F32),
            pltpu.VMEM((CONDS, NK * KF, 2 * KF), F32),
            pltpu.VMEM((UNITS, NK // 2, 128, 256), BF16),
            pltpu.VMEM((UNITS, NK // 2, 256, 256), BF16),
            pltpu.VMEM((5,) + block, F32),
            pltpu.VMEM((4, 4) + block, BF16),
            pltpu.VMEM(block, BF16),
            pltpu.VMEM((512, 512), BF16),
            pltpu.VMEM((512, 512), BF16),
            pltpu.VMEM(UNIT.shape, BF16),
            pltpu.SMEM((4, 128), jnp.int32),
            pltpu.SMEM((CONDS, NK), F32),
            pltpu.SMEM((CONDS,), F32),
            pltpu.SemaphoreType.DMA((12,)),
            pltpu.SemaphoreType.DMA((19,)),
            pltpu.SemaphoreType.DMA((19,)),
        ],
        compiler_params=pltpu.CompilerParams(
            collective_id=0, has_side_effects=True, vmem_limit_bytes=67043328 - 4 * 1024 * 1024
        ),
        name="gradient",
    )(counts.T, weights, thresholds, mask_param, target, kernels, edge, edge_t, unit)
    vmem = pl.BlockSpec(memory_space=pltpu.VMEM)
    plane = jax.ShapeDtypeStruct((1, 512, 512), F32)
    return pl.pallas_call(
        adjoint_kernel,
        out_shape=(plane, plane),
        in_specs=[vmem] * 4,
        out_specs=(any_space, any_space),
        scratch_shapes=[
            pltpu.VMEM((512, 512), BF16),
            pltpu.VMEM((512, 512), F32),
            pltpu.VMEM((512, 512), F32),
            pltpu.SemaphoreType.DMA((2, 4)),
        ],
        compiler_params=pltpu.CompilerParams(vmem_limit_bytes=16 * 1024 * 1024),
        name="adjoint",
    )(gspec, mask_param, edge, edge_t)


def solution(mesh):
    placed = (P("tiles", None, None), P("tiles", None, None), P(), P(), P(), P())
    return jax.shard_map(
        shards,
        mesh=mesh,
        in_specs=placed,
        out_specs=(P("tiles", None, None), P("tiles", None, None)),
        check_vma=False,
    )
```

```python
import functools

import jax
import jax.numpy as jnp
import ml_dtypes
import numpy as np
from jax import lax
from jax.experimental import pallas as pl
from jax.experimental.pallas import tpu as pltpu
from jax.sharding import PartitionSpec as P

TILE = 256
HALO = 32
KF = 64
DEV_COLS = 8
PADDED = TILE + 2 * HALO
COARSE = 2 * KF
NK = 12
CONDS = 4
UNITS = 4
STEEPNESS = 8.0
STEP_SIZE = 0.25
SCALE = 1.0 / (PADDED * KF)

F32 = jnp.float32
BF16 = jnp.bfloat16
MESH = pl.DeviceIdType.MESH
WAYS = [(dr, dc) for dr in (-1, 0, 1) for dc in (-1, 0, 1) if (dr, dc) != (0, 0)]


def bf(values):
    return np.asarray(values, np.float32).astype(ml_dtypes.bfloat16)


def edge_table():
    freq = np.arange(KF) - KF // 2
    pixels = np.arange(PADDED)
    angles = 2.0 * np.pi * freq[:, None] * pixels[None, :] / PADDED
    forward = np.concatenate([np.cos(angles), np.sin(angles)], 0)
    table = np.zeros((2 * TILE, 4 * 2 * KF))
    for slot in range(4):
        first = (slot - 1) * TILE - HALO
        for pixel in range(2 * TILE):
            if 0 <= pixel - first < PADDED:
                table[pixel, slot * 2 * KF : (slot + 1) * 2 * KF] = forward[:, pixel - first]
    return bf(table)


def unit_tables():
    freq = np.arange(KF) - KF // 2
    angles = 2.0 * np.pi * np.arange(COARSE)[:, None] * freq[None, :] / COARSE
    cos_t, sin_t = np.cos(angles), np.sin(angles)
    t1 = np.block([[cos_t.T, sin_t.T], [-sin_t.T, cos_t.T]])
    t2 = np.block([[cos_t, -sin_t], [sin_t, cos_t]])
    shift = (np.arange(TILE) + HALO)[:, None] - PADDED / COARSE * np.arange(COARSE)[None, :]
    waves = np.arange(1, COARSE // 2)
    interp = (
        1.0 + 2.0 * np.cos(2.0 * np.pi * shift[:, :, None] * waves / PADDED).sum(-1)
    ) / COARSE
    up_hi = bf(interp)
    up_lo = bf(interp - up_hi.astype(np.float64))
    return np.concatenate(
        [
            bf(t1),
            bf(t2.T),
            up_hi.T,
            np.concatenate([up_hi, up_lo], 1),
            np.concatenate([up_hi.T, up_lo.T], 0),
            np.concatenate([bf(t2), bf(t1.T)], 1),
        ],
        0,
    )


STAGES = (
    ("mix", 1, 123, 150),
    ("field", NK // 2, 53, 250),
    ("rows", 1, 70, 250),
    ("resist", 1, 70, 400),
    ("down", 1, 53, 200),
    ("coarse", 1, 53, 250),
    ("half", NK // 2, 53, 200),
    ("gather", 1, 141, 0),
)


def unit_order(units):
    at = [[0, 0, 0.0] for _ in range(units)]
    clock, order = 0.0, []
    while any(stage < len(STAGES) for stage, _, _ in at):
        alive = [u for u in range(units) if at[u][0] < len(STAGES)]
        u = next((u for u in alive if at[u][2] <= clock), None)
        if u is None:
            clock = min(at[u][2] for u in alive)
            continue
        stage, j, _ = at[u]
        name, steps, length, wait = STAGES[stage]
        order.append((u, name, j))
        clock += length
        if j + 1 < steps:
            at[u][1] = j + 1
        else:
            at[u] = [stage + 1, 0, clock + wait]
    return order


ORDER = unit_order(UNITS)
EDGE = edge_table()
EDGE_T = np.ascontiguousarray(EDGE.T)
UNIT = unit_tables()


def dot(a, b):
    return jnp.dot(a, b, preferred_element_type=F32)


def swap_pair(v):
    return jnp.concatenate(
        [
            jnp.concatenate([v[:64, :128], v[64:, :128]], 1),
            jnp.concatenate([v[:64, 128:], v[64:, 128:]], 1),
        ],
        0,
    )


def low_half(shape):
    return lax.broadcasted_iota(jnp.int32, shape, 1) < KF


def gradient_kernel(
    counts_in, weights_in, thresholds_in, mask, target, kernels, edge, edge_t, unit,
    out,
    levels, halves, part, got, spec, tgt, kraw, kre, kim, row_halves, fields, acc, gspec, shared, edge_v, edge_tv, unit_v, counts, weights, thresholds,
    load_sem, send_sem, recv_sem,
):
    me = lax.axis_index("tiles")
    devices = lax.axis_size("tiles")
    quarter = devices // 4
    half = devices // 2
    my_col = me % DEV_COLS
    my_row = me // DEV_COLS
    grid_rows = devices // DEV_COLS
    heavy = me < half
    partner = me + (3 - 2 * (me // quarter)) * quarter

    def has(dr, dc):
        ok = (my_row + dr >= 0) & (my_row + dr < grid_rows)
        return ok & (my_col + dc >= 0) & (my_col + dc < DEV_COLS)

    def peer(dr, dc):
        return lax.rem(me + dr * DEV_COLS + dc + devices, devices)

    order = (0, 3, 1, 2)
    first_loads = [
        pltpu.make_async_copy(
            mask.at[0, pl.ds(r * 128, 128)], levels.at[pl.ds(r * 128, 128)], load_sem.at[12 + r]
        )
        for r in range(4)
    ]
    loads = [
        None,
        pltpu.make_async_copy(edge, edge_v, load_sem.at[1]),
        pltpu.make_async_copy(edge_t, edge_tv, load_sem.at[2]),
        pltpu.make_async_copy(kernels, kraw, load_sem.at[3]),
        pltpu.make_async_copy(unit, unit_v, load_sem.at[4]),
        pltpu.make_async_copy(counts_in, counts, load_sem.at[9]),
        pltpu.make_async_copy(thresholds_in, thresholds, load_sem.at[10]),
        pltpu.make_async_copy(weights_in, weights, load_sem.at[11]),
    ] + [
        pltpu.make_async_copy(
            target.at[0, pl.ds((k // 2) * TILE, TILE), pl.ds((k % 2) * TILE, TILE)],
            tgt.at[k],
            load_sem.at[5 + k],
        )
        for k in range(4)
    ]
    first_loads[0].start()
    first_loads[3].start()
    loads[1].start()
    first_loads[1].start()
    first_loads[2].start()
    loads[2].start()

    barrier = pltpu.get_barrier_semaphore()
    greeted = jnp.int32(1)
    for dr, dc in WAYS:
        greeted = greeted + has(dr, dc).astype(jnp.int32)

        @pl.when(has(dr, dc))
        def _():
            pl.semaphore_signal(barrier, inc=1, device_id=(peer(dr, dc),), device_id_type=MESH)

    pl.semaphore_signal(barrier, inc=1, device_id=(partner,), device_id_type=MESH)

    def remote(src, dst, number, to):
        return pltpu.make_async_remote_copy(
            src_ref=src,
            dst_ref=dst,
            send_sem=send_sem.at[number],
            recv_sem=recv_sem.at[number],
            device_id=(to,),
            device_id_type=MESH,
        )

    span = {-1: 0, 0: pl.ds(1, 2), 1: 3}
    back = {-1: 3, 0: pl.ds(1, 2), 1: 0}
    rim = {-1: 1, 0: pl.ds(1, 2), 1: 2}

    def spectrum_copy(number):
        dr, dc = WAYS[number]
        return remote(part.at[span[dr], span[dc]], got.at[back[dr], back[dc]], number, peer(dr, dc))

    def gradient_copies(k):
        a, e = k // 2, k % 2
        dr, dc = 2 * a - 1, 2 * e - 1
        ways = ((dr, 0), (0, dc), (dr, dc))
        slots = ((back[dr], 1 + e), (1 + a, back[dc]), (back[dr], back[dc]))
        return [
            (way, remote(gspec.at[1 + a, 1 + e], gspec.at[slot], 9 + 3 * k + n, peer(*way)))
            for n, (way, slot) in enumerate(zip(ways, slots))
        ]

    def publish(k):
        for way, copy in gradient_copies(k):

            @pl.when(has(*way))
            def _():
                copy.start()

    target_copy = remote(
        target.at[0, pl.ds(TILE, TILE), pl.ds(TILE, TILE)], tgt.at[4], 21, partner
    )
    share_copy = remote(spec.at[3], spec.at[4], 8, partner)
    result_copy = remote(shared, gspec.at[2, 2], 22, partner)

    for dr, dc in WAYS:

        @pl.when(jnp.logical_not(has(dr, dc)))
        def _():
            rows = 2 if dr == 0 else 1
            cols = 2 if dc == 0 else 1
            for i in range(rows):
                for j in range(cols):
                    a = {-1: 0, 0: 1 + i, 1: 3}[dr]
                    e = {-1: 0, 0: 1 + j, 1: 3}[dc]
                    got[a, e] = jnp.zeros((KF, 2 * KF), BF16)
                    gspec[a, e] = jnp.zeros((KF, 2 * KF), BF16)

    low = low_half((KF, 2 * KF))
    tall = {0: slice(0, 128), 1: slice(0, 384), 2: slice(128, 512), 3: slice(384, 512)}

    def products(a):
        prod = dot(edge_tv[a * 128 : (a + 1) * 128, tall[a]], halves[tall[a], :])
        for e in range(4):
            top = prod[:KF, e * 128 : (e + 1) * 128]
            low_rows = pltpu.roll(prod[KF:, e * 128 : (e + 1) * 128], KF, 1)
            value = jnp.where(low, top - low_rows, -(top + low_rows))
            if a in (1, 2) and e in (1, 2):
                acc[(a - 1) * 2 + e - 1] = value
            else:
                part[a, e] = value.astype(BF16)

    def send_spectra(step):
        for number, (dr, dc) in enumerate(WAYS):
            if dr == step:

                @pl.when(has(dr, dc))
                def _():
                    spectrum_copy(number).start()

    for r in order:
        rows = slice(r * 128, (r + 1) * 128)
        first_loads[r].wait()
        x = jnp.tanh(0.5 * levels[rows, :]).astype(BF16)
        if r == 0:
            loads[1].wait()
        halves[rows, 0:128] = dot(x[:, 0:128], edge_v[0:128, 0:128]).astype(BF16)
        halves[rows, 128:384] = dot(x, edge_v[:, 128:384]).astype(BF16)
        halves[rows, 384:512] = dot(x[:, 384:512], edge_v[384:512, 384:512]).astype(BF16)
        if r == 0:
            loads[2].wait()
            for load in loads[3:]:
                load.start()
            products(0)
            pl.semaphore_wait(barrier, greeted)
            send_spectra(-1)
        if r == 3:
            products(3)
            send_spectra(1)
    products(1)
    products(2)
    send_spectra(0)

    loads[3].wait()
    loads[7].wait()

    @pl.loop(0, CONDS)
    def _(c):
        for n in range(NK):
            k = kraw[c, n]
            amount = jnp.sqrt(jnp.full((1, 2 * KF), weights[c, n], F32)) * SCALE
            k = k * amount
            turned = pltpu.roll(k, KF, 1)
            kre[c, n * KF : (n + 1) * KF, :] = jnp.where(low, k, turned)
            kim[c, n * KF : (n + 1) * KF, :] = jnp.where(low, -turned, k)

    for load in loads[4:7] + loads[8:]:
        load.wait()

    for number, (dr, dc) in enumerate(WAYS):

        @pl.when(has(-dr, -dc))
        def _():
            spectrum_copy(number).wait_recv()

    for a in (1, 0):
        for e in (1, 0):
            oa = 3 * a
            oe = 3 * e
            total = (
                acc[a * 2 + e]
                + got[1 + a, oe].astype(F32)
                + got[oa, 1 + e].astype(F32)
                + got[oa, oe].astype(F32)
            )
            spec[a * 2 + e] = total.astype(BF16)
            acc[a * 2 + e] = jnp.zeros((KF, 2 * KF), F32)

        if a == 1:

            @pl.when(heavy)
            def _():
                target_copy.start()
                share_copy.start()

    acc[4] = jnp.zeros((KF, 2 * KF), F32)

    t1 = unit_v.at[0:128, :]
    t2t = unit_v.at[128:256, :]
    upt = unit_v.at[256:384, :]
    up2 = unit_v.at[384:640, :]
    upt2 = unit_v.at[640:896, :]
    t2 = unit_v.at[896:1152, 0:128]
    t1t = unit_v.at[896:1152, 128:256]
    up = unit_v.at[384:640, 0:128]

    def mix(slot, tile, cond):
        s = spec[tile].astype(F32)
        turned = pltpu.roll(s, KF, 1)
        s2 = jnp.concatenate([s, s], 0)
        r2 = jnp.concatenate([turned, turned], 0)
        for j in range(NK // 2):
            rows = slice(j * 128, (j + 1) * 128)
            mixed = (kre[cond, rows, :] * s2 + kim[cond, rows, :] * r2).astype(BF16)
            row_halves[slot, j] = swap_pair(dot(mixed, t1[...]).astype(BF16))

    def field(slot, j, intensity):
        value = dot(t2[...], row_halves[slot, j])
        fields[slot, j] = value.astype(BF16)
        square = value * value
        square = square[:128] + square[128:]
        square = square[:, :128] + square[:, 128:]
        return square if intensity is None else intensity + square

    def interpolate_rows(intensity):
        hi = intensity.astype(BF16)
        return dot(up2[...], jnp.concatenate([hi, hi], 0))

    def resist_gradient(cols, tile, cond):
        hi = cols.astype(BF16)
        full = dot(jnp.concatenate([hi, hi], 1), upt2[...])
        tau = jnp.tanh((0.5 * STEEPNESS) * (full - thresholds[cond]))
        grad_int = 4.0 * (1.0 + tau - 2.0 * tgt[tile].astype(F32)) * (1.0 - tau * tau)
        return grad_int.astype(BF16)

    def coarse_rows(grad_int):
        return dot(upt[...], grad_int).astype(BF16)

    def coarse_gradient(down, live):
        return jnp.where(live, dot(down, up[...]), 0.0).astype(BF16)

    def grad_halves(slot, j, coarse):
        wide = jnp.concatenate([coarse, coarse], 1)
        value = fields[slot, j]
        grad_field = jnp.concatenate([value[:128] * wide, value[128:] * wide], 0)
        row_halves[slot, j] = swap_pair(dot(t2t[...], grad_field).astype(BF16))

    def gather(slot, tile, cond):
        sum_re = None
        for j in range(NK // 2):
            rows = slice(j * 128, (j + 1) * 128)
            grad_mix = dot(row_halves[slot, j], t1t[...])
            term_re = kre[cond, rows, :] * grad_mix
            term_im = kim[cond, rows, :] * grad_mix
            sum_re = term_re if j == 0 else sum_re + term_re
            sum_im = term_im if j == 0 else sum_im + term_im
        total = sum_re[:KF] + sum_re[KF:] + pltpu.roll(sum_im[:KF] + sum_im[KF:], KF, 1)
        acc[tile] = acc[tile] + total

    def pick(test, a, b):
        return jnp.where(test, a, b).astype(jnp.int32)

    def unit_group(i, carry):
        @pl.when(jnp.logical_not(heavy) & (i == 1))
        def _():
            target_copy.wait_recv()
            share_copy.wait_recv()

        own = jnp.logical_not(heavy) & (i == 0)
        tile = pick(heavy, i, 4)
        tiles = [pick(own, u, tile) for u in range(UNITS)]
        conds = [pick(own, 0, u) for u in range(UNITS)]
        lives = [
            cond < counts[pick(tile == 4, 3, tile), pick(tile == 4, partner, me)]
            for tile, cond in zip(tiles, conds)
        ]
        args = list(zip(tiles, conds))
        state = [{"bright": None} for _ in range(UNITS)]

        def emit(u, stage, j):
            now = state[u]
            if stage == "mix":
                mix(u, *args[u])
            elif stage == "field":
                now["bright"] = field(u, j, now["bright"])
            elif stage == "rows":
                now["cols"] = interpolate_rows(now["bright"])
            elif stage == "resist":
                now["grad"] = resist_gradient(now["cols"], *args[u])
            elif stage == "down":
                now["down"] = coarse_rows(now["grad"])
            elif stage == "coarse":
                now["coarse"] = coarse_gradient(now["down"], lives[u])
            elif stage == "half":
                grad_halves(u, j, now["coarse"])
            else:
                gather(u, *args[u])

        for step in ORDER:
            emit(*step)

        @pl.when(jnp.logical_not(heavy) & (i == 1))
        def _():
            shared[...] = acc[4].astype(BF16)
            result_copy.start()

        for k in range(4):

            @pl.when(pick(heavy, pick(i == k, 1, 0) * (1 if k < 3 else 0), pick(i == 0, 1, 0)) == 1)
            def _():
                gspec[1 + k // 2, 1 + k % 2] = acc[k].astype(BF16)
                publish(k)

        return carry

    lax.fori_loop(0, jnp.where(heavy, 3, 2), unit_group, jnp.int32(0))

    @pl.when(heavy)
    def _():
        result_copy.wait_recv()
        publish(3)
        share_copy.wait_send()
        target_copy.wait_send()

    @pl.when(jnp.logical_not(heavy))
    def _():
        result_copy.wait_send()

    for number, (dr, dc) in enumerate(WAYS):

        @pl.when(has(dr, dc))
        def _():
            spectrum_copy(number).wait_send()

    for k in range(4):
        for (dr, dc), copy in gradient_copies(k):

            @pl.when(has(dr, dc))
            def _():
                copy.wait_send()

            @pl.when(has(-dr, -dc))
            def _():
                copy.wait_recv()

    out[...] = gspec[...]


def adjoint_kernel(gspec, mask, edge, edge_t, levels_out, gradient_out, whole, levels, gradient, sem):
    low = low_half((KF, 2 * KF))

    def unfold(a):
        for e in range(4):
            g = gspec[a, e].astype(F32)
            cols = slice(e * 128, (e + 1) * 128)
            whole[a * 128 : a * 128 + KF, cols] = jnp.where(low, g, -g).astype(BF16)
            whole[a * 128 + KF : (a + 1) * 128, cols] = (-pltpu.roll(g, KF, 1)).astype(BF16)

    copies = []
    for r in range(4):
        for a in {0: (0, 1), 1: (2,), 2: (), 3: (3,)}[r]:
            unfold(a)
        rows = slice(r * 128, (r + 1) * 128)
        start = ((r + 1) // 2) * 128
        halves = dot(edge[rows, start : start + 256], whole[start : start + 256, :]).astype(BF16)
        for cols, tall in (
            (slice(0, 128), slice(0, 256)),
            (slice(128, 384), slice(128, 384)),
            (slice(384, 512), slice(256, 512)),
        ):
            canvas = dot(halves[:, tall], edge_t[tall, cols])
            before = mask[0, rows, cols]
            transmit = jnp.tanh(0.5 * before)
            grad = canvas * (0.5 - 0.5 * transmit * transmit)
            gradient[rows, cols] = grad
            levels[rows, cols] = before - STEP_SIZE * grad
        for k, (source, out) in enumerate(((gradient, gradient_out), (levels, levels_out))):
            copy = pltpu.make_async_copy(source.at[rows], out.at[0, rows], sem.at[k, r])
            copy.start()
            copies.append(copy)
    for copy in copies:
        copy.wait()


def shards(mask_param, target, counts, kernels, weights, thresholds):
    edge = jnp.asarray(EDGE)
    edge_t = jnp.asarray(EDGE_T)
    unit = jnp.asarray(UNIT)
    any_space = pl.BlockSpec(memory_space=pltpu.HBM)
    block = (KF, 2 * KF)
    gspec = pl.pallas_call(
        gradient_kernel,
        out_shape=jax.ShapeDtypeStruct((4, 4) + block, BF16),
        in_specs=[any_space] * 9,
        out_specs=pl.BlockSpec(memory_space=pltpu.VMEM),
        scratch_shapes=[
            pltpu.VMEM((512, 512), F32),
            pltpu.VMEM((512, 512), BF16),
            pltpu.VMEM((4, 4) + block, BF16),
            pltpu.VMEM((4, 4) + block, BF16),
            pltpu.VMEM((5,) + block, BF16),
            pltpu.VMEM((5, TILE, TILE), BF16),
            pltpu.VMEM((CONDS, NK) + block, F32),
            pltpu.VMEM((CONDS, NK * KF, 2 * KF), F32),
            pltpu.VMEM((CONDS, NK * KF, 2 * KF), F32),
            pltpu.VMEM((UNITS, NK // 2, 128, 256), BF16),
            pltpu.VMEM((UNITS, NK // 2, 256, 256), BF16),
            pltpu.VMEM((5,) + block, F32),
            pltpu.VMEM((4, 4) + block, BF16),
            pltpu.VMEM(block, BF16),
            pltpu.VMEM((512, 512), BF16),
            pltpu.VMEM((512, 512), BF16),
            pltpu.VMEM(UNIT.shape, BF16),
            pltpu.SMEM((4, 128), jnp.int32),
            pltpu.SMEM((CONDS, NK), F32),
            pltpu.SMEM((CONDS,), F32),
            pltpu.SemaphoreType.DMA((16,)),
            pltpu.SemaphoreType.DMA((23,)),
            pltpu.SemaphoreType.DMA((23,)),
        ],
        compiler_params=pltpu.CompilerParams(
            collective_id=0, has_side_effects=True, vmem_limit_bytes=67043328 - 4 * 1024 * 1024
        ),
        name="gradient",
    )(counts.T, weights, thresholds, mask_param, target, kernels, edge, edge_t, unit)
    vmem = pl.BlockSpec(memory_space=pltpu.VMEM)
    plane = jax.ShapeDtypeStruct((1, 512, 512), F32)
    return pl.pallas_call(
        adjoint_kernel,
        out_shape=(plane, plane),
        in_specs=[vmem] * 4,
        out_specs=(any_space, any_space),
        scratch_shapes=[
            pltpu.VMEM((512, 512), BF16),
            pltpu.VMEM((512, 512), F32),
            pltpu.VMEM((512, 512), F32),
            pltpu.SemaphoreType.DMA((2, 4)),
        ],
        compiler_params=pltpu.CompilerParams(vmem_limit_bytes=16 * 1024 * 1024),
        name="adjoint",
    )(gspec, mask_param, edge, edge_t)


def solution(mesh):
    placed = (P("tiles", None, None), P("tiles", None, None), P(), P(), P(), P())
    return jax.shard_map(
        shards,
        mesh=mesh,
        in_specs=placed,
        out_specs=(P("tiles", None, None), P("tiles", None, None)),
        check_vma=False,
    )
```

```python
import functools

import jax
import jax.numpy as jnp
import ml_dtypes
import numpy as np
from jax import lax
from jax.experimental import pallas as pl
from jax.experimental.pallas import tpu as pltpu
from jax.sharding import PartitionSpec as P

TILE = 256
HALO = 32
KF = 64
DEV_COLS = 8
PADDED = TILE + 2 * HALO
COARSE = 2 * KF
NK = 12
CONDS = 4
UNITS = 4
STEEPNESS = 8.0
STEP_SIZE = 0.25
SCALE = 1.0 / (PADDED * KF)

F32 = jnp.float32
BF16 = jnp.bfloat16
MESH = pl.DeviceIdType.MESH
WAYS = [(dr, dc) for dr in (-1, 0, 1) for dc in (-1, 0, 1) if (dr, dc) != (0, 0)]


def bf(values):
    return np.asarray(values, np.float32).astype(ml_dtypes.bfloat16)


def edge_table():
    freq = np.arange(KF) - KF // 2
    pixels = np.arange(PADDED)
    angles = 2.0 * np.pi * freq[:, None] * pixels[None, :] / PADDED
    forward = np.concatenate([np.cos(angles), np.sin(angles)], 0)
    table = np.zeros((2 * TILE, 4 * 2 * KF))
    for slot in range(4):
        first = (slot - 1) * TILE - HALO
        for pixel in range(2 * TILE):
            if 0 <= pixel - first < PADDED:
                table[pixel, slot * 2 * KF : (slot + 1) * 2 * KF] = forward[:, pixel - first]
    return bf(table)


def unit_tables():
    freq = np.arange(KF) - KF // 2
    angles = 2.0 * np.pi * np.arange(COARSE)[:, None] * freq[None, :] / COARSE
    cos_t, sin_t = np.cos(angles), np.sin(angles)
    t1 = np.block([[cos_t.T, sin_t.T], [-sin_t.T, cos_t.T]])
    t2 = np.block([[cos_t, -sin_t], [sin_t, cos_t]])
    shift = (np.arange(TILE) + HALO)[:, None] - PADDED / COARSE * np.arange(COARSE)[None, :]
    waves = np.arange(1, COARSE // 2)
    interp = (
        1.0 + 2.0 * np.cos(2.0 * np.pi * shift[:, :, None] * waves / PADDED).sum(-1)
    ) / COARSE
    up_hi = bf(interp)
    up_lo = bf(interp - up_hi.astype(np.float64))
    return np.concatenate(
        [
            bf(t1),
            bf(t2.T),
            up_hi.T,
            np.concatenate([up_hi, up_lo], 1),
            np.concatenate([up_hi.T, up_lo.T], 0),
            np.concatenate([bf(t2), bf(t1.T)], 1),
        ],
        0,
    )


STAGES = (
    ("mix", 1, 123, 150),
    ("field", NK // 2, 53, 250),
    ("rows", 1, 70, 250),
    ("resist", 1, 70, 400),
    ("down", 1, 53, 200),
    ("coarse", 1, 53, 250),
    ("half", NK // 2, 53, 200),
    ("gather", 1, 141, 0),
)


def unit_order(units):
    at = [[0, 0, 0.0] for _ in range(units)]
    clock, order = 0.0, []
    while any(stage < len(STAGES) for stage, _, _ in at):
        alive = [u for u in range(units) if at[u][0] < len(STAGES)]
        u = next((u for u in alive if at[u][2] <= clock), None)
        if u is None:
            clock = min(at[u][2] for u in alive)
            continue
        stage, j, _ = at[u]
        name, steps, length, wait = STAGES[stage]
        order.append((u, name, j))
        clock += length
        if j + 1 < steps:
            at[u][1] = j + 1
        else:
            at[u] = [stage + 1, 0, clock + wait]
    return order


ORDER = unit_order(UNITS)
EDGE = edge_table()
EDGE_T = np.ascontiguousarray(EDGE.T)
UNIT = unit_tables()


def dot(a, b):
    return jnp.dot(a, b, preferred_element_type=F32)


def swap_pair(v):
    return jnp.concatenate(
        [
            jnp.concatenate([v[:64, :128], v[64:, :128]], 1),
            jnp.concatenate([v[:64, 128:], v[64:, 128:]], 1),
        ],
        0,
    )


def low_half(shape):
    return lax.broadcasted_iota(jnp.int32, shape, 1) < KF


def gradient_kernel(
    counts_in, weights_in, thresholds_in, mask, target, kernels, edge, edge_t, unit,
    out,
    levels, halves, part, got, spec, tgt, kraw, kre, kim, row_halves, fields, acc, gspec, shared, edge_v, edge_tv, unit_v, counts, weights, thresholds,
    load_sem, send_sem, recv_sem,
):
    me = lax.axis_index("tiles")
    devices = lax.axis_size("tiles")
    quarter = devices // 4
    half = devices // 2
    my_col = me % DEV_COLS
    my_row = me // DEV_COLS
    grid_rows = devices // DEV_COLS
    heavy = me < half
    partner = me + (3 - 2 * (me // quarter)) * quarter

    def has(dr, dc):
        ok = (my_row + dr >= 0) & (my_row + dr < grid_rows)
        return ok & (my_col + dc >= 0) & (my_col + dc < DEV_COLS)

    def peer(dr, dc):
        return lax.rem(me + dr * DEV_COLS + dc + devices, devices)

    order = (0, 3, 1, 2)
    first_loads = [
        pltpu.make_async_copy(
            mask.at[0, pl.ds(r * 128, 128)], levels.at[pl.ds(r * 128, 128)], load_sem.at[12 + r]
        )
        for r in range(4)
    ]
    loads = [
        None,
        pltpu.make_async_copy(edge, edge_v, load_sem.at[1]),
        pltpu.make_async_copy(edge_t, edge_tv, load_sem.at[2]),
        pltpu.make_async_copy(kernels, kraw, load_sem.at[3]),
        pltpu.make_async_copy(unit, unit_v, load_sem.at[4]),
        pltpu.make_async_copy(counts_in, counts, load_sem.at[9]),
        pltpu.make_async_copy(thresholds_in, thresholds, load_sem.at[10]),
        pltpu.make_async_copy(weights_in, weights, load_sem.at[11]),
    ] + [
        pltpu.make_async_copy(
            target.at[0, pl.ds((k // 2) * TILE, TILE), pl.ds((k % 2) * TILE, TILE)],
            tgt.at[k],
            load_sem.at[5 + k],
        )
        for k in range(4)
    ]
    first_loads[0].start()
    first_loads[3].start()
    loads[1].start()
    first_loads[1].start()
    first_loads[2].start()
    loads[2].start()

    barrier = pltpu.get_barrier_semaphore()
    greeted = jnp.int32(1)
    for dr, dc in WAYS:
        greeted = greeted + has(dr, dc).astype(jnp.int32)

        @pl.when(has(dr, dc))
        def _():
            pl.semaphore_signal(barrier, inc=1, device_id=(peer(dr, dc),), device_id_type=MESH)

    pl.semaphore_signal(barrier, inc=1, device_id=(partner,), device_id_type=MESH)

    def remote(src, dst, number, to):
        return pltpu.make_async_remote_copy(
            src_ref=src,
            dst_ref=dst,
            send_sem=send_sem.at[number],
            recv_sem=recv_sem.at[number],
            device_id=(to,),
            device_id_type=MESH,
        )

    span = {-1: 0, 0: pl.ds(1, 2), 1: 3}
    back = {-1: 3, 0: pl.ds(1, 2), 1: 0}
    rim = {-1: 1, 0: pl.ds(1, 2), 1: 2}

    def spectrum_copy(number):
        dr, dc = WAYS[number]
        return remote(part.at[span[dr], span[dc]], got.at[back[dr], back[dc]], number, peer(dr, dc))

    def gradient_copies(k):
        a, e = k // 2, k % 2
        dr, dc = 2 * a - 1, 2 * e - 1
        ways = ((dr, 0), (0, dc), (dr, dc))
        slots = ((back[dr], 1 + e), (1 + a, back[dc]), (back[dr], back[dc]))
        return [
            (way, remote(gspec.at[1 + a, 1 + e], gspec.at[slot], 9 + 3 * k + n, peer(*way)))
            for n, (way, slot) in enumerate(zip(ways, slots))
        ]

    def publish(k):
        for way, copy in gradient_copies(k):

            @pl.when(has(*way))
            def _():
                copy.start()

    target_copy = remote(
        target.at[0, pl.ds(TILE, TILE), pl.ds(TILE, TILE)], tgt.at[4], 21, partner
    )
    share_copy = remote(spec.at[3], spec.at[4], 8, partner)
    result_copy = remote(shared, gspec.at[2, 2], 22, partner)

    for dr, dc in WAYS:

        @pl.when(jnp.logical_not(has(dr, dc)))
        def _():
            rows = 2 if dr == 0 else 1
            cols = 2 if dc == 0 else 1
            for i in range(rows):
                for j in range(cols):
                    a = {-1: 0, 0: 1 + i, 1: 3}[dr]
                    e = {-1: 0, 0: 1 + j, 1: 3}[dc]
                    got[a, e] = jnp.zeros((KF, 2 * KF), BF16)
                    gspec[a, e] = jnp.zeros((KF, 2 * KF), BF16)

    low = low_half((KF, 2 * KF))
    tall = {0: slice(0, 128), 1: slice(0, 384), 2: slice(128, 512), 3: slice(384, 512)}

    def products(a):
        prod = dot(edge_tv[a * 128 : (a + 1) * 128, tall[a]], halves[tall[a], :])
        for e in range(4):
            top = prod[:KF, e * 128 : (e + 1) * 128]
            low_rows = pltpu.roll(prod[KF:, e * 128 : (e + 1) * 128], KF, 1)
            value = jnp.where(low, top - low_rows, -(top + low_rows))
            if a in (1, 2) and e in (1, 2):
                acc[(a - 1) * 2 + e - 1] = value
            else:
                part[a, e] = value.astype(BF16)

    def send_spectra(step):
        for number, (dr, dc) in enumerate(WAYS):
            if dr == step:

                @pl.when(has(dr, dc))
                def _():
                    spectrum_copy(number).start()

    for r in order:
        rows = slice(r * 128, (r + 1) * 128)
        first_loads[r].wait()
        x = jnp.tanh(0.5 * levels[rows, :]).astype(BF16)
        if r == 0:
            loads[1].wait()
        halves[rows, 0:128] = dot(x[:, 0:128], edge_v[0:128, 0:128]).astype(BF16)
        halves[rows, 128:384] = dot(x, edge_v[:, 128:384]).astype(BF16)
        halves[rows, 384:512] = dot(x[:, 384:512], edge_v[384:512, 384:512]).astype(BF16)
        if r == 0:
            loads[2].wait()
            for load in loads[3:]:
                load.start()
            products(0)
            pl.semaphore_wait(barrier, greeted)
            send_spectra(-1)
        if r == 3:
            products(3)
            send_spectra(1)
    products(1)
    products(2)
    send_spectra(0)

    loads[3].wait()
    loads[7].wait()

    @pl.loop(0, CONDS)
    def _(c):
        for n in range(NK):
            k = kraw[c, n]
            amount = jnp.sqrt(jnp.full((1, 2 * KF), weights[c, n], F32)) * SCALE
            k = k * amount
            turned = pltpu.roll(k, KF, 1)
            kre[c, n * KF : (n + 1) * KF, :] = jnp.where(low, k, turned)
            kim[c, n * KF : (n + 1) * KF, :] = jnp.where(low, -turned, k)

    for load in loads[4:7] + loads[8:]:
        load.wait()

    for number, (dr, dc) in enumerate(WAYS):

        @pl.when(has(-dr, -dc))
        def _():
            spectrum_copy(number).wait_recv()

    for a in (1, 0):
        for e in (1, 0):
            oa = 3 * a
            oe = 3 * e
            total = (
                acc[a * 2 + e]
                + got[1 + a, oe].astype(F32)
                + got[oa, 1 + e].astype(F32)
                + got[oa, oe].astype(F32)
            )
            spec[a * 2 + e] = total.astype(BF16)
            acc[a * 2 + e] = jnp.zeros((KF, 2 * KF), F32)

        if a == 1:

            @pl.when(heavy)
            def _():
                target_copy.start()
                share_copy.start()

    acc[4] = jnp.zeros((KF, 2 * KF), F32)

    t1 = unit_v.at[0:128, :]
    t2t = unit_v.at[128:256, :]
    upt = unit_v.at[256:384, :]
    up2 = unit_v.at[384:640, :]
    upt2 = unit_v.at[640:896, :]
    t2 = unit_v.at[896:1152, 0:128]
    t1t = unit_v.at[896:1152, 128:256]
    up = unit_v.at[384:640, 0:128]

    def mix(slot, tile, cond):
        s = spec[tile].astype(F32)
        turned = pltpu.roll(s, KF, 1)
        s2 = jnp.concatenate([s, s], 0)
        r2 = jnp.concatenate([turned, turned], 0)
        for j in range(NK // 2):
            rows = slice(j * 128, (j + 1) * 128)
            mixed = (kre[cond, rows, :] * s2 + kim[cond, rows, :] * r2).astype(BF16)
            row_halves[slot, j] = swap_pair(dot(mixed, t1[...]).astype(BF16))

    def field(slot, j, intensity):
        value = dot(t2[...], row_halves[slot, j])
        fields[slot, j] = value.astype(BF16)
        square = value * value
        square = square[:128] + square[128:]
        square = square[:, :128] + square[:, 128:]
        return square if intensity is None else intensity + square

    def interpolate_rows(intensity):
        hi = intensity.astype(BF16)
        return dot(up2[...], jnp.concatenate([hi, hi], 0))

    def resist_gradient(cols, tile, cond):
        hi = cols.astype(BF16)
        full = dot(jnp.concatenate([hi, hi], 1), upt2[...])
        tau = jnp.tanh((0.5 * STEEPNESS) * (full - thresholds[cond]))
        grad_int = 4.0 * (1.0 + tau - 2.0 * tgt[tile].astype(F32)) * (1.0 - tau * tau)
        return grad_int.astype(BF16)

    def coarse_rows(grad_int):
        return dot(upt[...], grad_int).astype(BF16)

    def coarse_gradient(down, live):
        return jnp.where(live, dot(down, up[...]), 0.0).astype(BF16)

    def grad_halves(slot, j, coarse):
        wide = jnp.concatenate([coarse, coarse], 1)
        value = fields[slot, j]
        grad_field = jnp.concatenate([value[:128] * wide, value[128:] * wide], 0)
        row_halves[slot, j] = swap_pair(dot(t2t[...], grad_field).astype(BF16))

    def gather(slot, tile, cond):
        sum_re = None
        for j in range(NK // 2):
            rows = slice(j * 128, (j + 1) * 128)
            grad_mix = dot(row_halves[slot, j], t1t[...])
            term_re = kre[cond, rows, :] * grad_mix
            term_im = kim[cond, rows, :] * grad_mix
            sum_re = term_re if j == 0 else sum_re + term_re
            sum_im = term_im if j == 0 else sum_im + term_im
        total = sum_re[:KF] + sum_re[KF:] + pltpu.roll(sum_im[:KF] + sum_im[KF:], KF, 1)
        acc[tile] = acc[tile] + total

    def pick(test, a, b):
        return jnp.where(test, a, b).astype(jnp.int32)

    def unit_group(i, carry):
        @pl.when(jnp.logical_not(heavy) & (i == 1))
        def _():
            target_copy.wait_recv()
            share_copy.wait_recv()

        own = jnp.logical_not(heavy) & (i == 0)
        tile = pick(heavy, i, 4)
        tiles = [pick(own, u, tile) for u in range(UNITS)]
        conds = [pick(own, 0, u) for u in range(UNITS)]
        lives = [
            cond < counts[pick(tile == 4, 3, tile), pick(tile == 4, partner, me)]
            for tile, cond in zip(tiles, conds)
        ]
        args = list(zip(tiles, conds))
        state = [{"bright": None} for _ in range(UNITS)]

        def emit(u, stage, j):
            now = state[u]
            if stage == "mix":
                mix(u, *args[u])
            elif stage == "field":
                now["bright"] = field(u, j, now["bright"])
            elif stage == "rows":
                now["cols"] = interpolate_rows(now["bright"])
            elif stage == "resist":
                now["grad"] = resist_gradient(now["cols"], *args[u])
            elif stage == "down":
                now["down"] = coarse_rows(now["grad"])
            elif stage == "coarse":
                now["coarse"] = coarse_gradient(now["down"], lives[u])
            elif stage == "half":
                grad_halves(u, j, now["coarse"])
            else:
                gather(u, *args[u])

        for step in ORDER:
            emit(*step)

        @pl.when(jnp.logical_not(heavy) & (i == 1))
        def _():
            shared[...] = acc[4].astype(BF16)
            result_copy.start()

        for k in range(4):

            @pl.when(pick(heavy, pick(i == k, 1, 0) * (1 if k < 3 else 0), pick(i == 0, 1, 0)) == 1)
            def _():
                gspec[1 + k // 2, 1 + k % 2] = acc[k].astype(BF16)
                publish(k)

        return carry

    lax.fori_loop(0, jnp.where(heavy, 3, 2), unit_group, jnp.int32(0))

    @pl.when(heavy)
    def _():
        result_copy.wait_recv()
        publish(3)
        share_copy.wait_send()
        target_copy.wait_send()

    @pl.when(jnp.logical_not(heavy))
    def _():
        result_copy.wait_send()

    for number, (dr, dc) in enumerate(WAYS):

        @pl.when(has(dr, dc))
        def _():
            spectrum_copy(number).wait_send()

    for k in range(4):
        for (dr, dc), copy in gradient_copies(k):

            @pl.when(has(dr, dc))
            def _():
                copy.wait_send()

            @pl.when(has(-dr, -dc))
            def _():
                copy.wait_recv()

    out[...] = gspec[...]


def adjoint_kernel(gspec, mask, edge, edge_t, levels_out, gradient_out, whole, levels, gradient, sem):
    low = low_half((KF, 2 * KF))

    def unfold(a):
        for e in range(4):
            g = gspec[a, e].astype(F32)
            cols = slice(e * 128, (e + 1) * 128)
            whole[a * 128 : a * 128 + KF, cols] = jnp.where(low, g, -g).astype(BF16)
            whole[a * 128 + KF : (a + 1) * 128, cols] = (-pltpu.roll(g, KF, 1)).astype(BF16)

    copies = []
    for r in range(4):
        for a in {0: (0, 1), 1: (2,), 2: (), 3: (3,)}[r]:
            unfold(a)
        rows = slice(r * 128, (r + 1) * 128)
        start = ((r + 1) // 2) * 128
        halves = dot(edge[rows, start : start + 256], whole[start : start + 256, :]).astype(BF16)
        for cols, tall in (
            (slice(0, 128), slice(0, 256)),
            (slice(128, 384), slice(128, 384)),
            (slice(384, 512), slice(256, 512)),
        ):
            canvas = dot(halves[:, tall], edge_t[tall, cols])
            before = mask[0, rows, cols]
            transmit = jnp.tanh(0.5 * before)
            grad = canvas * (0.5 - 0.5 * transmit * transmit)
            gradient[rows, cols] = grad
            levels[rows, cols] = before - STEP_SIZE * grad
        for k, (source, out) in enumerate(((gradient, gradient_out), (levels, levels_out))):
            copy = pltpu.make_async_copy(source.at[rows], out.at[0, rows], sem.at[k, r])
            copy.start()
            copies.append(copy)
    for copy in copies:
        copy.wait()


def shards(mask_param, target, counts, kernels, weights, thresholds):
    edge = jnp.asarray(EDGE)
    edge_t = jnp.asarray(EDGE_T)
    unit = jnp.asarray(UNIT)
    any_space = pl.BlockSpec(memory_space=pltpu.HBM)
    block = (KF, 2 * KF)
    gspec = pl.pallas_call(
        gradient_kernel,
        out_shape=pltpu.VMEM((4, 4) + block, BF16),
        in_specs=[any_space] * 9,
        out_specs=pl.BlockSpec(memory_space=pltpu.VMEM),
        scratch_shapes=[
            pltpu.VMEM((512, 512), F32),
            pltpu.VMEM((512, 512), BF16),
            pltpu.VMEM((4, 4) + block, BF16),
            pltpu.VMEM((4, 4) + block, BF16),
            pltpu.VMEM((5,) + block, BF16),
            pltpu.VMEM((5, TILE, TILE), BF16),
            pltpu.VMEM((CONDS, NK) + block, F32),
            pltpu.VMEM((CONDS, NK * KF, 2 * KF), F32),
            pltpu.VMEM((CONDS, NK * KF, 2 * KF), F32),
            pltpu.VMEM((UNITS, NK // 2, 128, 256), BF16),
            pltpu.VMEM((UNITS, NK // 2, 256, 256), BF16),
            pltpu.VMEM((5,) + block, F32),
            pltpu.VMEM((4, 4) + block, BF16),
            pltpu.VMEM(block, BF16),
            pltpu.VMEM((512, 512), BF16),
            pltpu.VMEM((512, 512), BF16),
            pltpu.VMEM(UNIT.shape, BF16),
            pltpu.SMEM((4, 128), jnp.int32),
            pltpu.SMEM((CONDS, NK), F32),
            pltpu.SMEM((CONDS,), F32),
            pltpu.SemaphoreType.DMA((16,)),
            pltpu.SemaphoreType.DMA((23,)),
            pltpu.SemaphoreType.DMA((23,)),
        ],
        compiler_params=pltpu.CompilerParams(
            collective_id=0, has_side_effects=True, vmem_limit_bytes=67043328 - 4 * 1024 * 1024
        ),
        name="gradient",
    )(*[pltpu.with_memory_space_constraint(x, pltpu.HBM) for x in (counts.T, weights, thresholds, mask_param, target, kernels, edge, edge_t, unit)])
    vmem = pl.BlockSpec(memory_space=pltpu.VMEM)
    plane = jax.ShapeDtypeStruct((1, 512, 512), F32)
    return pl.pallas_call(
        adjoint_kernel,
        out_shape=(plane, plane),
        in_specs=[vmem] * 4,
        out_specs=(any_space, any_space),
        scratch_shapes=[
            pltpu.VMEM((512, 512), BF16),
            pltpu.VMEM((512, 512), F32),
            pltpu.VMEM((512, 512), F32),
            pltpu.SemaphoreType.DMA((2, 4)),
        ],
        compiler_params=pltpu.CompilerParams(vmem_limit_bytes=16 * 1024 * 1024),
        name="adjoint",
    )(gspec, mask_param, edge, edge_t)


def solution(mesh):
    placed = (P("tiles", None, None), P("tiles", None, None), P(), P(), P(), P())
    return jax.shard_map(
        shards,
        mesh=mesh,
        in_specs=placed,
        out_specs=(P("tiles", None, None), P("tiles", None, None)),
        check_vma=False,
    )
```

```python
import functools

import jax
import jax.numpy as jnp
import ml_dtypes
import numpy as np
from jax import lax
from jax.experimental import pallas as pl
from jax.experimental.pallas import tpu as pltpu
from jax.sharding import PartitionSpec as P

TILE = 256
HALO = 32
KF = 64
DEV_COLS = 8
PADDED = TILE + 2 * HALO
COARSE = 2 * KF
NK = 12
CONDS = 4
UNITS = 4
STEEPNESS = 8.0
STEP_SIZE = 0.25
SCALE = 1.0 / (PADDED * KF)

F32 = jnp.float32
BF16 = jnp.bfloat16
MESH = pl.DeviceIdType.MESH
BEYOND = ((1, 0), (0, 1), (1, 1))
WAYS = [(dr, dc) for dr in (-1, 0, 1) for dc in (-1, 0, 1) if (dr, dc) != (0, 0)]


def bf(values):
    return np.asarray(values, np.float32).astype(ml_dtypes.bfloat16)


def edge_table():
    freq = np.arange(KF) - KF // 2
    pixels = np.arange(PADDED)
    angles = 2.0 * np.pi * freq[:, None] * pixels[None, :] / PADDED
    forward = np.concatenate([np.cos(angles), np.sin(angles)], 0)
    table = np.zeros((2 * TILE, 4 * 2 * KF))
    for slot in range(4):
        first = (slot - 1) * TILE - HALO
        for pixel in range(2 * TILE):
            if 0 <= pixel - first < PADDED:
                table[pixel, slot * 2 * KF : (slot + 1) * 2 * KF] = forward[:, pixel - first]
    return bf(table)


def unit_tables():
    freq = np.arange(KF) - KF // 2
    angles = 2.0 * np.pi * np.arange(COARSE)[:, None] * freq[None, :] / COARSE
    cos_t, sin_t = np.cos(angles), np.sin(angles)
    t1 = np.block([[cos_t.T, sin_t.T], [-sin_t.T, cos_t.T]])
    t2 = np.block([[cos_t, -sin_t], [sin_t, cos_t]])
    shift = (np.arange(TILE) + HALO)[:, None] - PADDED / COARSE * np.arange(COARSE)[None, :]
    waves = np.arange(1, COARSE // 2)
    interp = (
        1.0 + 2.0 * np.cos(2.0 * np.pi * shift[:, :, None] * waves / PADDED).sum(-1)
    ) / COARSE
    up_hi = bf(interp)
    up_lo = bf(interp - up_hi.astype(np.float64))
    return np.concatenate(
        [
            bf(t1),
            bf(t2.T),
            up_hi.T,
            np.concatenate([up_hi, up_lo], 1),
            np.concatenate([up_hi.T, up_lo.T], 0),
            np.concatenate([bf(t2), bf(t1.T)], 1),
        ],
        0,
    )


STAGES = (
    ("mix", 1, 123, 150),
    ("field", NK // 2, 53, 250),
    ("rows", 1, 70, 250),
    ("resist", 1, 70, 400),
    ("down", 1, 53, 200),
    ("coarse", 1, 53, 250),
    ("half", NK // 2, 53, 200),
    ("gather", 1, 141, 0),
)


def unit_order(units):
    at = [[0, 0, 0.0] for _ in range(units)]
    clock, order = 0.0, []
    while any(stage < len(STAGES) for stage, _, _ in at):
        alive = [u for u in range(units) if at[u][0] < len(STAGES)]
        u = next((u for u in alive if at[u][2] <= clock), None)
        if u is None:
            clock = min(at[u][2] for u in alive)
            continue
        stage, j, _ = at[u]
        name, steps, length, wait = STAGES[stage]
        order.append((u, name, j))
        clock += length
        if j + 1 < steps:
            at[u][1] = j + 1
        else:
            at[u] = [stage + 1, 0, clock + wait]
    return order


ORDER = unit_order(UNITS)
EDGE = edge_table()
EDGE_T = np.ascontiguousarray(EDGE.T)
UNIT = unit_tables()


def dot(a, b):
    return jnp.dot(a, b, preferred_element_type=F32)


def swap_pair(v):
    return jnp.concatenate(
        [
            jnp.concatenate([v[:64, :128], v[64:, :128]], 1),
            jnp.concatenate([v[:64, 128:], v[64:, 128:]], 1),
        ],
        0,
    )


def low_half(shape):
    return lax.broadcasted_iota(jnp.int32, shape, 1) < KF


def gradient_kernel(
    counts_in, weights_in, thresholds_in, mask, target, kernels, edge, edge_t, unit,
    out,
    levels, halves, part, got, spec, tgt, kraw, kre, kim, row_halves, fields, acc, gspec, shared, edge_v, edge_tv, unit_v, counts, weights, thresholds,
    load_sem, send_sem, recv_sem,
):
    me = lax.axis_index("tiles")
    devices = lax.axis_size("tiles")
    quarter = devices // 4
    half = devices // 2
    my_col = me % DEV_COLS
    my_row = me // DEV_COLS
    grid_rows = devices // DEV_COLS
    heavy = me < half

    def partner_of(device):
        return device + (3 - 2 * (device // quarter)) * quarter

    partner = partner_of(me)

    def has(dr, dc):
        ok = (my_row + dr >= 0) & (my_row + dr < grid_rows)
        return ok & (my_col + dc >= 0) & (my_col + dc < DEV_COLS)

    def partner_has(dr, dc):
        ok = (partner // DEV_COLS + dr < grid_rows) & (partner % DEV_COLS + dc < DEV_COLS)
        return jnp.logical_not(heavy) & ok

    def peer(dr, dc):
        return lax.rem(me + dr * DEV_COLS + dc + devices, devices)

    barrier = pltpu.get_barrier_semaphore()
    greeted = jnp.int32(1)
    for dr, dc in WAYS:
        greeted = greeted + has(dr, dc).astype(jnp.int32)

        @pl.when(has(dr, dc))
        def _():
            pl.semaphore_signal(barrier, inc=1, device_id=(peer(dr, dc),), device_id_type=MESH)

    pl.semaphore_signal(barrier, inc=1, device_id=(partner,), device_id_type=MESH)
    for dr, dc in BEYOND:
        greeted = greeted + partner_has(dr, dc).astype(jnp.int32)
        owner = me - dr * DEV_COLS - dc

        @pl.when(has(-dr, -dc) & (owner < half))
        def _():
            pl.semaphore_signal(
                barrier, inc=1, device_id=(partner_of(owner),), device_id_type=MESH
            )


    order = (0, 3, 1, 2)
    first_loads = [
        pltpu.make_async_copy(
            mask.at[0, pl.ds(r * 128, 128)], levels.at[pl.ds(r * 128, 128)], load_sem.at[12 + r]
        )
        for r in range(4)
    ]
    loads = [
        None,
        pltpu.make_async_copy(edge, edge_v, load_sem.at[1]),
        pltpu.make_async_copy(edge_t, edge_tv, load_sem.at[2]),
        pltpu.make_async_copy(kernels, kraw, load_sem.at[3]),
        pltpu.make_async_copy(unit, unit_v, load_sem.at[4]),
        pltpu.make_async_copy(counts_in, counts, load_sem.at[9]),
        pltpu.make_async_copy(thresholds_in, thresholds, load_sem.at[10]),
        pltpu.make_async_copy(weights_in, weights, load_sem.at[11]),
    ] + [
        pltpu.make_async_copy(
            target.at[0, pl.ds((k // 2) * TILE, TILE), pl.ds((k % 2) * TILE, TILE)],
            tgt.at[k],
            load_sem.at[5 + k],
        )
        for k in range(4)
    ]
    first_loads[0].start()
    first_loads[3].start()
    loads[1].start()
    first_loads[1].start()
    first_loads[2].start()
    loads[2].start()

    def remote(src, dst, number, to):
        return pltpu.make_async_remote_copy(
            src_ref=src,
            dst_ref=dst,
            send_sem=send_sem.at[number],
            recv_sem=recv_sem.at[number],
            device_id=(to,),
            device_id_type=MESH,
        )

    span = {-1: 0, 0: pl.ds(1, 2), 1: 3}
    back = {-1: 3, 0: pl.ds(1, 2), 1: 0}
    rim = {-1: 1, 0: pl.ds(1, 2), 1: 2}

    def spectrum_copy(number):
        dr, dc = WAYS[number]
        return remote(part.at[span[dr], span[dc]], got.at[back[dr], back[dc]], number, peer(dr, dc))

    def gradient_copies(k):
        a, e = k // 2, k % 2
        dr, dc = 2 * a - 1, 2 * e - 1
        ways = ((dr, 0), (0, dc), (dr, dc))
        slots = ((back[dr], 1 + e), (1 + a, back[dc]), (back[dr], back[dc]))
        return [
            (way, remote(gspec.at[1 + a, 1 + e], gspec.at[slot], 9 + 3 * k + n, peer(*way)))
            for n, (way, slot) in enumerate(zip(ways, slots))
        ]

    def publish(k):
        for way, copy in gradient_copies(k):

            @pl.when(has(*way))
            def _():
                copy.start()

    target_copy = remote(
        target.at[0, pl.ds(TILE, TILE), pl.ds(TILE, TILE)], tgt.at[4], 21, partner
    )
    share_copy = remote(spec.at[3], spec.at[4], 8, partner)
    result_copy = remote(shared, gspec.at[2, 2], 22, partner)
    result_copies = [
        (
            way,
            pltpu.make_async_remote_copy(
                src_ref=shared,
                dst_ref=gspec.at[slot],
                send_sem=send_sem.at[23 + n],
                recv_sem=recv_sem.at[18 + n],
                device_id=(lax.rem(partner + way[0] * DEV_COLS + way[1], devices),),
                device_id_type=MESH,
            ),
        )
        for n, (way, slot) in enumerate(zip(BEYOND, ((0, 2), (2, 0), (0, 0))))
    ]

    low = low_half((KF, 2 * KF))
    tall = {0: slice(0, 128), 1: slice(0, 384), 2: slice(128, 512), 3: slice(384, 512)}

    def products(a):
        prod = dot(edge_tv[a * 128 : (a + 1) * 128, tall[a]], halves[tall[a], :])
        for e in range(4):
            top = prod[:KF, e * 128 : (e + 1) * 128]
            low_rows = pltpu.roll(prod[KF:, e * 128 : (e + 1) * 128], KF, 1)
            value = jnp.where(low, top - low_rows, -(top + low_rows))
            if a in (1, 2) and e in (1, 2):
                acc[(a - 1) * 2 + e - 1] = value
            else:
                part[a, e] = value.astype(BF16)

    def send_spectra(step):
        for number, (dr, dc) in enumerate(WAYS):
            if dr == step:

                @pl.when(has(dr, dc))
                def _():
                    spectrum_copy(number).start()

    for r in order:
        rows = slice(r * 128, (r + 1) * 128)
        first_loads[r].wait()
        x = jnp.tanh(0.5 * levels[rows, :]).astype(BF16)
        if r == 0:
            loads[1].wait()
        halves[rows, 0:128] = dot(x[:, 0:128], edge_v[0:128, 0:128]).astype(BF16)
        halves[rows, 128:384] = dot(x, edge_v[:, 128:384]).astype(BF16)
        halves[rows, 384:512] = dot(x[:, 384:512], edge_v[384:512, 384:512]).astype(BF16)
        if r == 0:
            loads[2].wait()
            for load in loads[3:]:
                load.start()
            products(0)
            pl.semaphore_wait(barrier, greeted)
            send_spectra(-1)
        if r == 3:
            products(3)
            send_spectra(1)
    products(1)
    products(2)
    send_spectra(0)

    for dr, dc in WAYS:

        @pl.when(jnp.logical_not(has(dr, dc)))
        def _():
            rows = 2 if dr == 0 else 1
            cols = 2 if dc == 0 else 1
            for i in range(rows):
                for j in range(cols):
                    a = {-1: 0, 0: 1 + i, 1: 3}[dr]
                    e = {-1: 0, 0: 1 + j, 1: 3}[dc]
                    got[a, e] = jnp.zeros((KF, 2 * KF), BF16)
                    gspec[a, e] = jnp.zeros((KF, 2 * KF), BF16)

    loads[3].wait()
    loads[7].wait()

    @pl.loop(0, CONDS)
    def _(c):
        for n in range(NK):
            k = kraw[c, n]
            amount = jnp.sqrt(jnp.full((1, 2 * KF), weights[c, n], F32)) * SCALE
            k = k * amount
            turned = pltpu.roll(k, KF, 1)
            kre[c, n * KF : (n + 1) * KF, :] = jnp.where(low, k, turned)
            kim[c, n * KF : (n + 1) * KF, :] = jnp.where(low, -turned, k)

    for load in loads[4:7] + loads[8:]:
        load.wait()

    for number, (dr, dc) in enumerate(WAYS):

        @pl.when(has(-dr, -dc))
        def _():
            spectrum_copy(number).wait_recv()

    for a in (1, 0):
        for e in (1, 0):
            oa = 3 * a
            oe = 3 * e
            total = (
                acc[a * 2 + e]
                + got[1 + a, oe].astype(F32)
                + got[oa, 1 + e].astype(F32)
                + got[oa, oe].astype(F32)
            )
            spec[a * 2 + e] = total.astype(BF16)
            acc[a * 2 + e] = jnp.zeros((KF, 2 * KF), F32)

        if a == 1:

            @pl.when(heavy)
            def _():
                target_copy.start()
                share_copy.start()

    acc[4] = jnp.zeros((KF, 2 * KF), F32)

    t1 = unit_v.at[0:128, :]
    t2t = unit_v.at[128:256, :]
    upt = unit_v.at[256:384, :]
    up2 = unit_v.at[384:640, :]
    upt2 = unit_v.at[640:896, :]
    t2 = unit_v.at[896:1152, 0:128]
    t1t = unit_v.at[896:1152, 128:256]
    up = unit_v.at[384:640, 0:128]

    def mix(slot, tile, cond):
        s = spec[tile].astype(F32)
        turned = pltpu.roll(s, KF, 1)
        s2 = jnp.concatenate([s, s], 0)
        r2 = jnp.concatenate([turned, turned], 0)
        for j in range(NK // 2):
            rows = slice(j * 128, (j + 1) * 128)
            mixed = (kre[cond, rows, :] * s2 + kim[cond, rows, :] * r2).astype(BF16)
            row_halves[slot, j] = swap_pair(dot(mixed, t1[...]).astype(BF16))

    def field(slot, j, intensity):
        value = dot(t2[...], row_halves[slot, j])
        fields[slot, j] = value.astype(BF16)
        square = value * value
        square = square[:128] + square[128:]
        square = square[:, :128] + square[:, 128:]
        return square if intensity is None else intensity + square

    def interpolate_rows(intensity):
        hi = intensity.astype(BF16)
        return dot(up2[...], jnp.concatenate([hi, hi], 0))

    def resist_gradient(cols, tile, cond):
        hi = cols.astype(BF16)
        full = dot(jnp.concatenate([hi, hi], 1), upt2[...])
        tau = jnp.tanh((0.5 * STEEPNESS) * (full - thresholds[cond]))
        grad_int = 4.0 * (1.0 + tau - 2.0 * tgt[tile].astype(F32)) * (1.0 - tau * tau)
        return grad_int.astype(BF16)

    def coarse_rows(grad_int):
        return dot(upt[...], grad_int).astype(BF16)

    def coarse_gradient(down, live):
        return jnp.where(live, dot(down, up[...]), 0.0).astype(BF16)

    def grad_halves(slot, j, coarse):
        wide = jnp.concatenate([coarse, coarse], 1)
        value = fields[slot, j]
        grad_field = jnp.concatenate([value[:128] * wide, value[128:] * wide], 0)
        row_halves[slot, j] = swap_pair(dot(t2t[...], grad_field).astype(BF16))

    def gather(slot, tile, cond):
        sum_re = None
        for j in range(NK // 2):
            rows = slice(j * 128, (j + 1) * 128)
            grad_mix = dot(row_halves[slot, j], t1t[...])
            term_re = kre[cond, rows, :] * grad_mix
            term_im = kim[cond, rows, :] * grad_mix
            term_re = term_re[:KF] + term_re[KF:]
            term_im = term_im[:KF] + term_im[KF:]
            sum_re = term_re if j == 0 else sum_re + term_re
            sum_im = term_im if j == 0 else sum_im + term_im
        acc[tile] = acc[tile] + (sum_re + pltpu.roll(sum_im, KF, 1))

    def pick(test, a, b):
        return jnp.where(test, a, b).astype(jnp.int32)

    def unit_group(i, carry):
        @pl.when(jnp.logical_not(heavy) & (i == 1))
        def _():
            target_copy.wait_recv()
            share_copy.wait_recv()

        own = jnp.logical_not(heavy) & (i == 0)
        tile = pick(heavy, i, 4)
        tiles = [pick(own, u, tile) for u in range(UNITS)]
        conds = [pick(own, 0, u) for u in range(UNITS)]
        lives = [
            cond < counts[pick(tile == 4, 3, tile), pick(tile == 4, partner, me)]
            for tile, cond in zip(tiles, conds)
        ]
        args = list(zip(tiles, conds))
        state = [{"bright": None} for _ in range(UNITS)]

        def emit(u, stage, j):
            now = state[u]
            if stage == "mix":
                mix(u, *args[u])
            elif stage == "field":
                now["bright"] = field(u, j, now["bright"])
            elif stage == "rows":
                now["cols"] = interpolate_rows(now["bright"])
            elif stage == "resist":
                now["grad"] = resist_gradient(now["cols"], *args[u])
            elif stage == "down":
                now["down"] = coarse_rows(now["grad"])
            elif stage == "coarse":
                now["coarse"] = coarse_gradient(now["down"], lives[u])
            elif stage == "half":
                grad_halves(u, j, now["coarse"])
            else:
                gather(u, *args[u])

        for step in ORDER:
            emit(*step)

        @pl.when(jnp.logical_not(heavy) & (i == 1))
        def _():
            shared[...] = acc[4].astype(BF16)
            result_copy.start()
            for way, copy in result_copies:

                @pl.when(partner_has(*way))
                def _():
                    copy.start()


        for k in range(4):

            @pl.when(pick(heavy, pick(i == k, 1, 0) * (1 if k < 3 else 0), pick(i == 0, 1, 0)) == 1)
            def _():
                gspec[1 + k // 2, 1 + k % 2] = acc[k].astype(BF16)
                publish(k)

        return carry

    lax.fori_loop(0, jnp.where(heavy, 3, 2), unit_group, jnp.int32(0))

    @pl.when(heavy)
    def _():
        result_copy.wait_recv()
        share_copy.wait_send()
        target_copy.wait_send()

    @pl.when(jnp.logical_not(heavy))
    def _():
        result_copy.wait_send()
        for way, copy in result_copies:

            @pl.when(partner_has(*way))
            def _():
                copy.wait_send()


    for number, (dr, dc) in enumerate(WAYS):

        @pl.when(has(dr, dc))
        def _():
            spectrum_copy(number).wait_send()

    for k in range(4):
        for (dr, dc), copy in gradient_copies(k):

            @pl.when(has(dr, dc) & jnp.logical_not(heavy) if k == 3 else has(dr, dc))
            def _():
                copy.wait_send()

            @pl.when(has(-dr, -dc))
            def _():
                copy.wait_recv()

    out[...] = gspec[...]


def adjoint_kernel(gspec, mask, edge, edge_t, levels_out, gradient_out, whole, levels, gradient, sem):
    low = low_half((KF, 2 * KF))

    def unfold(a):
        for e in range(4):
            g = gspec[a, e].astype(F32)
            cols = slice(e * 128, (e + 1) * 128)
            whole[a * 128 : a * 128 + KF, cols] = jnp.where(low, g, -g).astype(BF16)
            whole[a * 128 + KF : (a + 1) * 128, cols] = (-pltpu.roll(g, KF, 1)).astype(BF16)

    copies = []
    for r in range(4):
        for a in {0: (0, 1), 1: (2,), 2: (), 3: (3,)}[r]:
            unfold(a)
        rows = slice(r * 128, (r + 1) * 128)
        start = ((r + 1) // 2) * 128
        halves = dot(edge[rows, start : start + 256], whole[start : start + 256, :]).astype(BF16)
        for cols, tall in (
            (slice(0, 128), slice(0, 256)),
            (slice(128, 384), slice(128, 384)),
            (slice(384, 512), slice(256, 512)),
        ):
            canvas = dot(halves[:, tall], edge_t[tall, cols])
            before = mask[0, rows, cols]
            transmit = jnp.tanh(0.5 * before)
            grad = canvas * (0.5 - 0.5 * transmit * transmit)
            gradient[rows, cols] = grad
            levels[rows, cols] = before - STEP_SIZE * grad
        for k, (source, out) in enumerate(((gradient, gradient_out), (levels, levels_out))):
            copy = pltpu.make_async_copy(source.at[rows], out.at[0, rows], sem.at[k, r])
            copy.start()
            copies.append(copy)
    for copy in copies:
        copy.wait()


def shards(mask_param, target, counts, kernels, weights, thresholds):
    edge = jnp.asarray(EDGE)
    edge_t = jnp.asarray(EDGE_T)
    unit = jnp.asarray(UNIT)
    any_space = pl.BlockSpec(memory_space=pltpu.HBM)
    block = (KF, 2 * KF)
    gspec = pl.pallas_call(
        gradient_kernel,
        out_shape=pltpu.VMEM((4, 4) + block, BF16),
        in_specs=[any_space] * 9,
        out_specs=pl.BlockSpec(memory_space=pltpu.VMEM),
        scratch_shapes=[
            pltpu.VMEM((512, 512), F32),
            pltpu.VMEM((512, 512), BF16),
            pltpu.VMEM((4, 4) + block, BF16),
            pltpu.VMEM((4, 4) + block, BF16),
            pltpu.VMEM((5,) + block, BF16),
            pltpu.VMEM((5, TILE, TILE), BF16),
            pltpu.VMEM((CONDS, NK) + block, F32),
            pltpu.VMEM((CONDS, NK * KF, 2 * KF), F32),
            pltpu.VMEM((CONDS, NK * KF, 2 * KF), F32),
            pltpu.VMEM((UNITS, NK // 2, 128, 256), BF16),
            pltpu.VMEM((UNITS, NK // 2, 256, 256), BF16),
            pltpu.VMEM((5,) + block, F32),
            pltpu.VMEM((4, 4) + block, BF16),
            pltpu.VMEM(block, BF16),
            pltpu.VMEM((512, 512), BF16),
            pltpu.VMEM((512, 512), BF16),
            pltpu.VMEM(UNIT.shape, BF16),
            pltpu.SMEM((4, 128), jnp.int32),
            pltpu.SMEM((CONDS, NK), F32),
            pltpu.SMEM((CONDS,), F32),
            pltpu.SemaphoreType.DMA((16,)),
            pltpu.SemaphoreType.DMA((26,)),
            pltpu.SemaphoreType.DMA((23,)),
        ],
        compiler_params=pltpu.CompilerParams(
            collective_id=0, has_side_effects=True, vmem_limit_bytes=67043328 - 4 * 1024 * 1024
        ),
        name="gradient",
    )(*[pltpu.with_memory_space_constraint(x, pltpu.HBM) for x in (counts.T, weights, thresholds, mask_param, target, kernels, edge, edge_t, unit)])
    vmem = pl.BlockSpec(memory_space=pltpu.VMEM)
    plane = jax.ShapeDtypeStruct((1, 512, 512), F32)
    return pl.pallas_call(
        adjoint_kernel,
        out_shape=(plane, plane),
        in_specs=[vmem] * 4,
        out_specs=(any_space, any_space),
        scratch_shapes=[
            pltpu.VMEM((512, 512), BF16),
            pltpu.VMEM((512, 512), F32),
            pltpu.VMEM((512, 512), F32),
            pltpu.SemaphoreType.DMA((2, 4)),
        ],
        compiler_params=pltpu.CompilerParams(vmem_limit_bytes=16 * 1024 * 1024),
        name="adjoint",
    )(gspec, mask_param, edge, edge_t)


def solution(mesh):
    placed = (P("tiles", None, None), P("tiles", None, None), P(), P(), P(), P())
    return jax.shard_map(
        shards,
        mesh=mesh,
        in_specs=placed,
        out_specs=(P("tiles", None, None), P("tiles", None, None)),
        check_vma=False,
    )
```

```python
import functools

import jax
import jax.numpy as jnp
import ml_dtypes
import numpy as np
from jax import lax
from jax.experimental import pallas as pl
from jax.experimental.pallas import tpu as pltpu
from jax.sharding import PartitionSpec as P

TILE = 256
HALO = 32
KF = 64
DEV_COLS = 8
PADDED = TILE + 2 * HALO
COARSE = 2 * KF
NK = 12
CONDS = 4
UNITS = 4
STEEPNESS = 8.0
STEP_SIZE = 0.25
SCALE = 1.0 / (PADDED * KF)

F32 = jnp.float32
BF16 = jnp.bfloat16
MESH = pl.DeviceIdType.MESH
BEYOND = ((1, 0), (0, 1), (1, 1))
WAYS = [(dr, dc) for dr in (-1, 0, 1) for dc in (-1, 0, 1) if (dr, dc) != (0, 0)]


def bf(values):
    return np.asarray(values, np.float32).astype(ml_dtypes.bfloat16)


def edge_table():
    freq = np.arange(KF) - KF // 2
    pixels = np.arange(PADDED)
    angles = 2.0 * np.pi * freq[:, None] * pixels[None, :] / PADDED
    forward = np.concatenate([np.cos(angles), np.sin(angles)], 0)
    table = np.zeros((2 * TILE, 4 * 2 * KF))
    for slot in range(4):
        first = (slot - 1) * TILE - HALO
        for pixel in range(2 * TILE):
            if 0 <= pixel - first < PADDED:
                table[pixel, slot * 2 * KF : (slot + 1) * 2 * KF] = forward[:, pixel - first]
    return bf(table)


def unit_tables():
    freq = np.arange(KF) - KF // 2
    angles = 2.0 * np.pi * np.arange(COARSE)[:, None] * freq[None, :] / COARSE
    cos_t, sin_t = np.cos(angles), np.sin(angles)
    t1 = np.block([[cos_t.T, sin_t.T], [-sin_t.T, cos_t.T]])
    t2 = np.block([[cos_t, -sin_t], [sin_t, cos_t]])
    shift = (np.arange(TILE) + HALO)[:, None] - PADDED / COARSE * np.arange(COARSE)[None, :]
    waves = np.arange(1, COARSE // 2)
    interp = (
        1.0 + 2.0 * np.cos(2.0 * np.pi * shift[:, :, None] * waves / PADDED).sum(-1)
    ) / COARSE
    up_hi = bf(interp)
    up_lo = bf(interp - up_hi.astype(np.float64))
    return np.concatenate(
        [
            bf(t1),
            bf(t2.T),
            up_hi.T,
            np.concatenate([up_hi, up_lo], 1),
            np.concatenate([up_hi.T, up_lo.T], 0),
            np.concatenate([bf(t2), bf(t1.T)], 1),
        ],
        0,
    )


STAGES = (
    ("mix", 1, 123, 150),
    ("field", NK // 2, 53, 250),
    ("rows", 1, 70, 250),
    ("resist", 1, 70, 400),
    ("down", 1, 53, 200),
    ("coarse", 1, 53, 250),
    ("half", NK // 2, 53, 200),
    ("gather", 1, 141, 0),
)


def unit_order(units):
    at = [[0, 0, 0.0] for _ in range(units)]
    clock, order = 0.0, []
    while any(stage < len(STAGES) for stage, _, _ in at):
        alive = [u for u in range(units) if at[u][0] < len(STAGES)]
        u = next((u for u in alive if at[u][2] <= clock), None)
        if u is None:
            clock = min(at[u][2] for u in alive)
            continue
        stage, j, _ = at[u]
        name, steps, length, wait = STAGES[stage]
        order.append((u, name, j))
        clock += length
        if j + 1 < steps:
            at[u][1] = j + 1
        else:
            at[u] = [stage + 1, 0, clock + wait]
    return order


ORDER = unit_order(UNITS)
EDGE = edge_table()
EDGE_T = np.ascontiguousarray(EDGE.T)
UNIT = unit_tables()


def dot(a, b):
    return jnp.dot(a, b, preferred_element_type=F32)


def swap_pair(v):
    return jnp.concatenate(
        [
            jnp.concatenate([v[:64, :128], v[64:, :128]], 1),
            jnp.concatenate([v[:64, 128:], v[64:, 128:]], 1),
        ],
        0,
    )


def low_half(shape):
    return lax.broadcasted_iota(jnp.int32, shape, 1) < KF


def gradient_kernel(
    counts_in, weights_in, thresholds_in, mask, target, kernels, edge, edge_t, unit,
    out,
    levels, halves, part, got, spec, tgt, kraw, kre, kim, row_halves, fields, acc, gspec, shared, edge_v, edge_tv, unit_v, counts, weights, thresholds,
    load_sem, send_sem, recv_sem,
):
    me = lax.axis_index("tiles")
    devices = lax.axis_size("tiles")
    quarter = devices // 4
    half = devices // 2
    my_col = me % DEV_COLS
    my_row = me // DEV_COLS
    grid_rows = devices // DEV_COLS
    heavy = me < half

    def partner_of(device):
        return device + (3 - 2 * (device // quarter)) * quarter

    partner = partner_of(me)

    def has(dr, dc):
        ok = (my_row + dr >= 0) & (my_row + dr < grid_rows)
        return ok & (my_col + dc >= 0) & (my_col + dc < DEV_COLS)

    def partner_has(dr, dc):
        ok = (partner // DEV_COLS + dr < grid_rows) & (partner % DEV_COLS + dc < DEV_COLS)
        return jnp.logical_not(heavy) & ok

    def peer(dr, dc):
        return lax.rem(me + dr * DEV_COLS + dc + devices, devices)

    barrier = pltpu.get_barrier_semaphore()
    greeted = jnp.int32(1)
    for dr, dc in WAYS:
        greeted = greeted + has(dr, dc).astype(jnp.int32)

        @pl.when(has(dr, dc))
        def _():
            pl.semaphore_signal(barrier, inc=1, device_id=(peer(dr, dc),), device_id_type=MESH)

    pl.semaphore_signal(barrier, inc=1, device_id=(partner,), device_id_type=MESH)
    for dr, dc in BEYOND:
        greeted = greeted + partner_has(dr, dc).astype(jnp.int32)
        owner = me - dr * DEV_COLS - dc

        @pl.when(has(-dr, -dc) & (owner < half))
        def _():
            pl.semaphore_signal(
                barrier, inc=1, device_id=(partner_of(owner),), device_id_type=MESH
            )


    order = (0, 3, 1, 2)
    first_loads = [
        pltpu.make_async_copy(
            mask.at[0, pl.ds(r * 128, 128)], levels.at[pl.ds(r * 128, 128)], load_sem.at[12 + r]
        )
        for r in range(4)
    ]
    loads = [
        None,
        pltpu.make_async_copy(edge, edge_v, load_sem.at[1]),
        pltpu.make_async_copy(edge_t, edge_tv, load_sem.at[2]),
        pltpu.make_async_copy(kernels, kraw, load_sem.at[3]),
        pltpu.make_async_copy(unit, unit_v, load_sem.at[4]),
        pltpu.make_async_copy(counts_in, counts, load_sem.at[9]),
        pltpu.make_async_copy(thresholds_in, thresholds, load_sem.at[10]),
        pltpu.make_async_copy(weights_in, weights, load_sem.at[11]),
    ] + [
        pltpu.make_async_copy(
            target.at[0, pl.ds((k // 2) * TILE, TILE), pl.ds((k % 2) * TILE, TILE)],
            tgt.at[k],
            load_sem.at[5 + k],
        )
        for k in range(4)
    ]
    first_loads[0].start()
    first_loads[3].start()
    loads[1].start()
    first_loads[1].start()
    first_loads[2].start()
    loads[2].start()

    def remote(src, dst, number, to):
        return pltpu.make_async_remote_copy(
            src_ref=src,
            dst_ref=dst,
            send_sem=send_sem.at[number],
            recv_sem=recv_sem.at[number],
            device_id=(to,),
            device_id_type=MESH,
        )

    span = {-1: 0, 0: pl.ds(1, 2), 1: 3}
    back = {-1: 3, 0: pl.ds(1, 2), 1: 0}
    rim = {-1: 1, 0: pl.ds(1, 2), 1: 2}

    def spectrum_copy(number):
        dr, dc = WAYS[number]
        return remote(part.at[span[dr], span[dc]], got.at[back[dr], back[dc]], number, peer(dr, dc))

    def gradient_copies(k):
        a, e = k // 2, k % 2
        dr, dc = 2 * a - 1, 2 * e - 1
        ways = ((dr, 0), (0, dc), (dr, dc))
        slots = ((back[dr], 1 + e), (1 + a, back[dc]), (back[dr], back[dc]))
        return [
            (way, remote(gspec.at[1 + a, 1 + e], gspec.at[slot], 9 + 3 * k + n, peer(*way)))
            for n, (way, slot) in enumerate(zip(ways, slots))
        ]

    def publish(k):
        for way, copy in reversed(gradient_copies(k)):

            @pl.when(has(*way))
            def _():
                copy.start()

    target_copy = remote(
        target.at[0, pl.ds(TILE, TILE), pl.ds(TILE, TILE)], tgt.at[4], 21, partner
    )
    share_copy = remote(spec.at[3], spec.at[4], 8, partner)
    result_copy = remote(shared, gspec.at[2, 2], 22, partner)
    result_copies = [
        (
            way,
            pltpu.make_async_remote_copy(
                src_ref=shared,
                dst_ref=gspec.at[slot],
                send_sem=send_sem.at[23 + n],
                recv_sem=recv_sem.at[18 + n],
                device_id=(lax.rem(partner + way[0] * DEV_COLS + way[1], devices),),
                device_id_type=MESH,
            ),
        )
        for n, (way, slot) in enumerate(zip(BEYOND, ((0, 2), (2, 0), (0, 0))))
    ]

    low = low_half((KF, 2 * KF))
    tall = {0: slice(0, 128), 1: slice(0, 384), 2: slice(128, 512), 3: slice(384, 512)}

    def products(a):
        prod = dot(edge_tv[a * 128 : (a + 1) * 128, tall[a]], halves[tall[a], :])
        for e in range(4):
            top = prod[:KF, e * 128 : (e + 1) * 128]
            low_rows = pltpu.roll(prod[KF:, e * 128 : (e + 1) * 128], KF, 1)
            value = jnp.where(low, top - low_rows, -(top + low_rows))
            if a in (1, 2) and e in (1, 2):
                acc[(a - 1) * 2 + e - 1] = value
            else:
                part[a, e] = value.astype(BF16)

    def send_spectra(step):
        for number, (dr, dc) in sorted(enumerate(WAYS), key=lambda item: item[1][1] == 0):
            if dr == step:

                @pl.when(has(dr, dc))
                def _():
                    spectrum_copy(number).start()

    for r in order:
        rows = slice(r * 128, (r + 1) * 128)
        first_loads[r].wait()
        x = jnp.tanh(0.5 * levels[rows, :]).astype(BF16)
        if r == 0:
            loads[1].wait()
        halves[rows, 0:128] = dot(x[:, 0:128], edge_v[0:128, 0:128]).astype(BF16)
        halves[rows, 128:384] = dot(x, edge_v[:, 128:384]).astype(BF16)
        halves[rows, 384:512] = dot(x[:, 384:512], edge_v[384:512, 384:512]).astype(BF16)
        if r == 0:
            loads[2].wait()
            for load in loads[3:]:
                load.start()
            products(0)
            pl.semaphore_wait(barrier, greeted)
            send_spectra(-1)
        if r == 3:
            products(3)
            send_spectra(1)
    products(1)
    products(2)
    send_spectra(0)

    for dr, dc in WAYS:

        @pl.when(jnp.logical_not(has(dr, dc)))
        def _():
            rows = 2 if dr == 0 else 1
            cols = 2 if dc == 0 else 1
            for i in range(rows):
                for j in range(cols):
                    a = {-1: 0, 0: 1 + i, 1: 3}[dr]
                    e = {-1: 0, 0: 1 + j, 1: 3}[dc]
                    got[a, e] = jnp.zeros((KF, 2 * KF), BF16)
                    gspec[a, e] = jnp.zeros((KF, 2 * KF), BF16)

    loads[3].wait()
    loads[7].wait()

    @pl.loop(0, CONDS)
    def _(c):
        for n in range(NK):
            k = kraw[c, n]
            amount = jnp.sqrt(jnp.full((1, 2 * KF), weights[c, n], F32)) * SCALE
            k = k * amount
            turned = pltpu.roll(k, KF, 1)
            kre[c, n * KF : (n + 1) * KF, :] = jnp.where(low, k, turned)
            kim[c, n * KF : (n + 1) * KF, :] = jnp.where(low, -turned, k)

    for load in loads[4:7] + loads[8:]:
        load.wait()

    for number, (dr, dc) in enumerate(WAYS):

        @pl.when(has(-dr, -dc))
        def _():
            spectrum_copy(number).wait_recv()

    for a in (1, 0):
        for e in (1, 0):
            oa = 3 * a
            oe = 3 * e
            total = (
                acc[a * 2 + e]
                + got[1 + a, oe].astype(F32)
                + got[oa, 1 + e].astype(F32)
                + got[oa, oe].astype(F32)
            )
            spec[a * 2 + e] = total.astype(BF16)
            acc[a * 2 + e] = jnp.zeros((KF, 2 * KF), F32)

        if a == 1:

            @pl.when(heavy)
            def _():
                target_copy.start()
                share_copy.start()

    acc[4] = jnp.zeros((KF, 2 * KF), F32)

    t1 = unit_v.at[0:128, :]
    t2t = unit_v.at[128:256, :]
    upt = unit_v.at[256:384, :]
    up2 = unit_v.at[384:640, :]
    upt2 = unit_v.at[640:896, :]
    t2 = unit_v.at[896:1152, 0:128]
    t1t = unit_v.at[896:1152, 128:256]
    up = unit_v.at[384:640, 0:128]

    def mix(slot, tile, cond):
        s = spec[tile].astype(F32)
        turned = pltpu.roll(s, KF, 1)
        s2 = jnp.concatenate([s, s], 0)
        r2 = jnp.concatenate([turned, turned], 0)
        for j in range(NK // 2):
            rows = slice(j * 128, (j + 1) * 128)
            mixed = (kre[cond, rows, :] * s2 + kim[cond, rows, :] * r2).astype(BF16)
            row_halves[slot, j] = swap_pair(dot(mixed, t1[...]).astype(BF16))

    def field(slot, j, intensity):
        value = dot(t2[...], row_halves[slot, j])
        fields[slot, j] = value.astype(BF16)
        square = value * value
        square = square[:128] + square[128:]
        square = square[:, :128] + square[:, 128:]
        return square if intensity is None else intensity + square

    def interpolate_rows(intensity):
        hi = intensity.astype(BF16)
        return dot(up2[...], jnp.concatenate([hi, hi], 0))

    def resist_gradient(cols, tile, cond):
        hi = cols.astype(BF16)
        full = dot(jnp.concatenate([hi, hi], 1), upt2[...])
        tau = jnp.tanh((0.5 * STEEPNESS) * (full - thresholds[cond]))
        grad_int = 4.0 * (1.0 + tau - 2.0 * tgt[tile].astype(F32)) * (1.0 - tau * tau)
        return grad_int.astype(BF16)

    def coarse_rows(grad_int):
        return dot(upt[...], grad_int).astype(BF16)

    def coarse_gradient(down, live):
        return jnp.where(live, dot(down, up[...]), 0.0).astype(BF16)

    def grad_halves(slot, j, coarse):
        wide = jnp.concatenate([coarse, coarse], 1)
        value = fields[slot, j]
        grad_field = jnp.concatenate([value[:128] * wide, value[128:] * wide], 0)
        row_halves[slot, j] = swap_pair(dot(t2t[...], grad_field).astype(BF16))

    def gather(slot, tile, cond):
        sum_re = None
        for j in range(NK // 2):
            rows = slice(j * 128, (j + 1) * 128)
            grad_mix = dot(row_halves[slot, j], t1t[...])
            term_re = kre[cond, rows, :] * grad_mix
            term_im = kim[cond, rows, :] * grad_mix
            term_re = term_re[:KF] + term_re[KF:]
            term_im = term_im[:KF] + term_im[KF:]
            sum_re = term_re if j == 0 else sum_re + term_re
            sum_im = term_im if j == 0 else sum_im + term_im
        acc[tile] = acc[tile] + (sum_re + pltpu.roll(sum_im, KF, 1))

    def pick(test, a, b):
        return jnp.where(test, a, b).astype(jnp.int32)

    def unit_group(i, carry):
        @pl.when(jnp.logical_not(heavy) & (i == 1))
        def _():
            target_copy.wait_recv()
            share_copy.wait_recv()

        own = jnp.logical_not(heavy) & (i == 0)
        tile = pick(heavy, i, 4)
        tiles = [pick(own, u, tile) for u in range(UNITS)]
        conds = [pick(own, 0, u) for u in range(UNITS)]
        lives = [
            cond < counts[pick(tile == 4, 3, tile), pick(tile == 4, partner, me)]
            for tile, cond in zip(tiles, conds)
        ]
        args = list(zip(tiles, conds))
        state = [{"bright": None} for _ in range(UNITS)]

        def emit(u, stage, j):
            now = state[u]
            if stage == "mix":
                mix(u, *args[u])
            elif stage == "field":
                now["bright"] = field(u, j, now["bright"])
            elif stage == "rows":
                now["cols"] = interpolate_rows(now["bright"])
            elif stage == "resist":
                now["grad"] = resist_gradient(now["cols"], *args[u])
            elif stage == "down":
                now["down"] = coarse_rows(now["grad"])
            elif stage == "coarse":
                now["coarse"] = coarse_gradient(now["down"], lives[u])
            elif stage == "half":
                grad_halves(u, j, now["coarse"])
            else:
                gather(u, *args[u])

        for step in ORDER:
            emit(*step)

        @pl.when(jnp.logical_not(heavy) & (i == 1))
        def _():
            shared[...] = acc[4].astype(BF16)
            result_copy.start()
            for way, copy in result_copies:

                @pl.when(partner_has(*way))
                def _():
                    copy.start()


        for k in range(4):

            @pl.when(pick(heavy, pick(i == k, 1, 0) * (1 if k < 3 else 0), pick(i == 0, 1, 0)) == 1)
            def _():
                gspec[1 + k // 2, 1 + k % 2] = acc[k].astype(BF16)
                publish(k)

        return carry

    lax.fori_loop(0, jnp.where(heavy, 3, 2), unit_group, jnp.int32(0))

    @pl.when(heavy)
    def _():
        result_copy.wait_recv()
        share_copy.wait_send()
        target_copy.wait_send()

    @pl.when(jnp.logical_not(heavy))
    def _():
        result_copy.wait_send()
        for way, copy in result_copies:

            @pl.when(partner_has(*way))
            def _():
                copy.wait_send()


    for a in (1, 2):
        for e in (1, 2):
            out[a, e] = gspec[a, e]

    for number, (dr, dc) in enumerate(WAYS):

        @pl.when(has(dr, dc))
        def _():
            spectrum_copy(number).wait_send()

    for k in range(4):
        for (dr, dc), copy in gradient_copies(k):

            @pl.when(has(dr, dc) & jnp.logical_not(heavy) if k == 3 else has(dr, dc))
            def _():
                copy.wait_send()

            @pl.when(has(-dr, -dc))
            def _():
                copy.wait_recv()

    out[0] = gspec[0]
    out[3] = gspec[3]
    for a in (1, 2):
        out[a, 0] = gspec[a, 0]
        out[a, 3] = gspec[a, 3]


def adjoint_kernel(gspec, mask, edge, edge_t, levels_out, gradient_out, whole, levels, gradient, sem):
    low = low_half((KF, 2 * KF))

    def unfold(a):
        for e in range(4):
            g = gspec[a, e].astype(F32)
            cols = slice(e * 128, (e + 1) * 128)
            whole[a * 128 : a * 128 + KF, cols] = jnp.where(low, g, -g).astype(BF16)
            whole[a * 128 + KF : (a + 1) * 128, cols] = (-pltpu.roll(g, KF, 1)).astype(BF16)

    copies = []
    for r in range(4):
        for a in {0: (0, 1), 1: (2,), 2: (), 3: (3,)}[r]:
            unfold(a)
        rows = slice(r * 128, (r + 1) * 128)
        start = ((r + 1) // 2) * 128
        halves = dot(edge[rows, start : start + 256], whole[start : start + 256, :]).astype(BF16)
        for cols, tall in (
            (slice(0, 128), slice(0, 256)),
            (slice(128, 384), slice(128, 384)),
            (slice(384, 512), slice(256, 512)),
        ):
            canvas = dot(halves[:, tall], edge_t[tall, cols])
            before = mask[0, rows, cols]
            transmit = jnp.tanh(0.5 * before)
            grad = canvas * (0.5 - 0.5 * transmit * transmit)
            gradient[rows, cols] = grad
            levels[rows, cols] = before - STEP_SIZE * grad
        for k, (source, out) in enumerate(((gradient, gradient_out), (levels, levels_out))):
            copy = pltpu.make_async_copy(source.at[rows], out.at[0, rows], sem.at[k, r])
            copy.start()
            copies.append(copy)
    for copy in copies:
        copy.wait()


def shards(mask_param, target, counts, kernels, weights, thresholds):
    edge = jnp.asarray(EDGE)
    edge_t = jnp.asarray(EDGE_T)
    unit = jnp.asarray(UNIT)
    any_space = pl.BlockSpec(memory_space=pltpu.HBM)
    block = (KF, 2 * KF)
    gspec = pl.pallas_call(
        gradient_kernel,
        out_shape=pltpu.VMEM((4, 4) + block, BF16),
        in_specs=[any_space] * 9,
        out_specs=pl.BlockSpec(memory_space=pltpu.VMEM),
        scratch_shapes=[
            pltpu.VMEM((512, 512), F32),
            pltpu.VMEM((512, 512), BF16),
            pltpu.VMEM((4, 4) + block, BF16),
            pltpu.VMEM((4, 4) + block, BF16),
            pltpu.VMEM((5,) + block, BF16),
            pltpu.VMEM((5, TILE, TILE), BF16),
            pltpu.VMEM((CONDS, NK) + block, F32),
            pltpu.VMEM((CONDS, NK * KF, 2 * KF), F32),
            pltpu.VMEM((CONDS, NK * KF, 2 * KF), F32),
            pltpu.VMEM((UNITS, NK // 2, 128, 256), BF16),
            pltpu.VMEM((UNITS, NK // 2, 256, 256), BF16),
            pltpu.VMEM((5,) + block, F32),
            pltpu.VMEM((4, 4) + block, BF16),
            pltpu.VMEM(block, BF16),
            pltpu.VMEM((512, 512), BF16),
            pltpu.VMEM((512, 512), BF16),
            pltpu.VMEM(UNIT.shape, BF16),
            pltpu.SMEM((4, 128), jnp.int32),
            pltpu.SMEM((CONDS, NK), F32),
            pltpu.SMEM((CONDS,), F32),
            pltpu.SemaphoreType.DMA((16,)),
            pltpu.SemaphoreType.DMA((26,)),
            pltpu.SemaphoreType.DMA((23,)),
        ],
        compiler_params=pltpu.CompilerParams(
            collective_id=0, has_side_effects=True, vmem_limit_bytes=67043328 - 4 * 1024 * 1024
        ),
        name="gradient",
    )(*[pltpu.with_memory_space_constraint(x, pltpu.HBM) for x in (counts.T, weights, thresholds, mask_param, target, kernels, edge, edge_t, unit)])
    vmem = pl.BlockSpec(memory_space=pltpu.VMEM)
    plane = jax.ShapeDtypeStruct((1, 512, 512), F32)
    return pl.pallas_call(
        adjoint_kernel,
        out_shape=(plane, plane),
        in_specs=[vmem] * 4,
        out_specs=(any_space, any_space),
        scratch_shapes=[
            pltpu.VMEM((512, 512), BF16),
            pltpu.VMEM((512, 512), F32),
            pltpu.VMEM((512, 512), F32),
            pltpu.SemaphoreType.DMA((2, 4)),
        ],
        compiler_params=pltpu.CompilerParams(vmem_limit_bytes=16 * 1024 * 1024),
        name="adjoint",
    )(gspec, mask_param, edge, edge_t)


def solution(mesh):
    placed = (P("tiles", None, None), P("tiles", None, None), P(), P(), P(), P())
    return jax.shard_map(
        shards,
        mesh=mesh,
        in_specs=placed,
        out_specs=(P("tiles", None, None), P("tiles", None, None)),
        check_vma=False,
    )
```
